32 devices in a mesh: grp: 2 (over x), pb: 8 (over z, y), row: 2 (over core).
Axes of the slice: x: 2, y: 2, z: 4, core: 2. Of those that a mesh axis runs over, the one named last changes fastest.
Arguments:
- record: float32 [4096, 1024], P(('grp', 'pb', 'row')), parts along dimension 0, may hold values from -12 to 12
- record_tail: float32 [254, 1024], P('grp'), parts along dimension 0, may hold values from -12 to 12
- projection: float32 [1024, 16], replicated, may hold values from -0.1875 to 0.1875
- window_start: int32 [2], P('grp'), parts along dimension 0, may hold values from 0 to 64
Outputs:
- row_profile: float32 [4096], P(('grp', 'pb', 'row')), parts along dimension 0
- col_profile: float32 [4096], P(('grp', 'pb', 'row')), parts along dimension 0
The draws below stay inside these ranges and needn't reach their ends.
There are 2 independent parts, one for each index of `grp`. The reference program is written for one: setup_inputs(seed, part) draws one part's arguments, and reference() takes and returns one part's arrays. A program takes and returns all parts, laid end to end along the dimension named above; an argument that names none is the same for every part. Nothing has to cross between parts.
All inputs are finite; a program needn't handle non-finite values.
Results may differ from the reference program's by a relative error of at most 0.0003.
Values sent between devices are 32-bit elements; how exact they have to be, the bound alone decides.
No kernel may reach another device: no remote copies, remote signals or barrier semaphores. Data moves between devices by JAX's collectives and lax.ppermute only.
A program may use at most 64 MiB of HBM per device.

```python
import math
import jax
import jax.numpy as jnp
from jax import lax

C = 1024
K = 16
M = 64
N = 2048
HEAD = 127


def make_signal(key):
    base = jax.random.fold_in(key, 7)
    noise_key, drive_key = jax.random.split(base, 2)
    total_rows = N + HEAD
    noise = jax.random.normal(noise_key, (total_rows, C), jnp.float32)
    drive = 0.3 * jax.random.normal(drive_key, (total_rows, C), jnp.float32)

    def advance(state_now, step_input):
        state_next = 0.98 * state_now + step_input
        return (state_next, state_next)
    final_state, drift = lax.scan(advance, jnp.zeros((C,), jnp.float32), drive)
    return jnp.clip(noise + drift, -12.0, 12.0)


def draw_record(key, part):
    return make_signal(key)[:N]


def draw_record_tail(key, part):
    return make_signal(key)[N:]


def centred(stream_key, extent, scale, reach, kind=jnp.bfloat16):
    return jnp.clip(scale * jax.random.normal(stream_key, extent, jnp.float32), -reach, reach).astype(kind)


def setup_inputs(seed: int = 0, part: int = 0) -> dict:
    arg_keys = jax.random.split(jax.random.key(seed), 5)
    own_keys = jax.random.split(jax.random.fold_in(arg_keys[4], part), 5)
    return {
        "record": draw_record(jax.random.fold_in(jax.random.fold_in(arg_keys[4], part), 71), part),
        "record_tail": draw_record_tail(jax.random.fold_in(jax.random.fold_in(arg_keys[4], part), 71), part),
        "projection": centred(arg_keys[2], (C, K), C ** -0.5, 0.1875, jnp.float32),
        "window_start": jax.random.randint(own_keys[3], (1,), 0, M + 1).astype(jnp.int32),
    }


epsilon = 1e-05
ceiling = 4.0

def zscores(window, count_rows):
    hankel = jnp.stack([window[..., offset:offset + count_rows, :] for offset in range(M)], axis=-2)
    center = lax.optimization_barrier(jnp.mean(hankel, axis=-2, keepdims=True))
    spread = lax.optimization_barrier(jnp.mean(jnp.square(hankel - center), axis=-2, keepdims=True))
    scaled = (hankel - center) * lax.rsqrt(spread + epsilon) * (1.0 / math.sqrt(M * hankel.shape[-1]))
    return scaled.astype(jnp.bfloat16)

def reference(record, record_tail, projection, window_start):
    joined = jnp.concatenate([record, record_tail], axis=0)
    projected = jnp.dot(joined, projection, precision=lax.Precision.HIGHEST, preferred_element_type=jnp.float32)
    total_rows = record.shape[0]
    start_row = window_start[0].astype(jnp.int32)
    series = lax.dynamic_slice_in_dim(projected, start_row, total_rows + M - 1, 0)
    scores = zscores(series, total_rows).reshape(total_rows, -1).astype(jnp.float32)
    exclusion = M // 4
    block_rows = math.gcd(512, total_rows)
    column_index = jnp.arange(total_rows, dtype=jnp.int32)

    def one_block(block_id):
        queries = lax.dynamic_slice_in_dim(scores, block_id * block_rows, block_rows, 0)
        distance = 2.0 - 2.0 * jnp.dot(queries, scores.T, precision=lax.Precision.HIGHEST, preferred_element_type=jnp.float32)
        row_index = block_id * block_rows + jnp.arange(block_rows, dtype=jnp.int32)
        separation = column_index[None, :] - row_index[:, None]
        later_min = lax.optimization_barrier(jnp.min(jnp.where(separation > exclusion, distance, ceiling), axis=1))
        earlier_min = lax.optimization_barrier(jnp.min(jnp.where(separation < -exclusion, distance, ceiling), axis=1))
        return (later_min, earlier_min)
    later_all, earlier_all = lax.map(one_block, jnp.arange(total_rows // block_rows, dtype=jnp.int32))
    return (later_all.reshape(total_rows), earlier_all.reshape(total_rows))
```

```python
import functools

import jax
import jax.numpy as jnp
from jax import lax
from jax.experimental import pallas as pl
from jax.experimental.pallas import tpu as pltpu
from jax.sharding import PartitionSpec as P

M = 64
LANES = 128
SUB = 8
epsilon = 1e-05
ceiling = 4.0
AXES = ("pb", "row")


def project_kernel(x_ref, p_ref, o_ref, y_ref):
    dims = p_ref.shape[0]
    per = LANES // dims
    rows = x_ref.shape[0]
    total = o_ref.shape[0] * per
    if rows != total:
        y_ref[...] = jnp.zeros_like(y_ref)
    y_ref[:rows, :] = lax.dot_general(
        x_ref[...],
        p_ref[...],
        (((1,), (1,)), ((), ())),
        precision=lax.Precision.HIGHEST,
        preferred_element_type=jnp.float32,
    )
    for u in range(per):
        o_ref[:, u * dims : (u + 1) * dims] = y_ref[pl.ds(u, total // per, stride=per), :]


def project(x, p_t):
    dims = p_t.shape[0]
    per = LANES // dims
    out_rows = -(-x.shape[0] // per)
    return pl.pallas_call(
        project_kernel,
        out_shape=jax.ShapeDtypeStruct((out_rows, LANES), jnp.float32),
        in_specs=[pl.BlockSpec(memory_space=pltpu.VMEM)] * 2,
        out_specs=pl.BlockSpec(memory_space=pltpu.VMEM),
        scratch_shapes=[pltpu.VMEM((out_rows * per, dims), jnp.float32)],
        name="project",
    )(x, p_t)


def profile_kernel(cfg, start_ref, *refs):
    masks, dims, rows, n_blocks = cfg
    pieces = refs[: len(masks)]
    tail_ref, after_ref, before_ref = refs[len(masks) : len(masks) + 3]
    s_ref, x_ref, c_ref, r_ref, own_ref, ownb_ref, sc_ref = refs[len(masks) + 3 :]
    per = LANES // dims
    steps = M // per
    brows = rows // per
    all_rows = n_blocks * brows
    chunk = min(256, all_rows)
    seg = chunk // SUB
    n_chunks = all_rows // chunk
    n_x = (seg + steps + 2) * SUB
    me = lax.axis_index(AXES[0]) * lax.axis_size(AXES[1]) + lax.axis_index(AXES[1])

    for piece, piece_masks in zip(pieces, masks):
        for n, mask in enumerate(piece_masks):
            at = pl.multiple_of((me ^ mask) * brows, brows)
            s_ref[pl.ds(at, brows), :] = piece[n * brows : (n + 1) * brows, :]
    trows = tail_ref.shape[0]
    s_ref[all_rows : all_rows + trows, :] = tail_ref[...]
    pad = s_ref.shape[0] - all_rows - trows
    s_ref[all_rows + trows :, :] = jnp.zeros((pad, LANES), jnp.float32)

    start = start_ref[0]
    skip_rows = start // per
    skip = lax.rem(start, per) * dims

    def shift(first, second, lanes):
        lane = lax.broadcasted_iota(jnp.int32, first.shape, 1)
        return jnp.where(lane < LANES - lanes, first, second)

    def build(base):
        tiles = [
            s_ref[pl.ds(base + skip_rows + j, SUB, stride=seg), :] for j in range(seg + steps + 3)
        ]
        z = pltpu.roll(jnp.concatenate(tiles, axis=0), lax.rem(LANES - skip, LANES), 1)
        x = shift(z[:-SUB], z[SUB:], skip)
        x_ref[0] = x
        for b in range(1, per):
            y = pltpu.roll(x, LANES - b * dims, 1)
            x_ref[b, : n_x - SUB, :] = shift(y[:-SUB], y[SUB:], b * dims)
        total, dev, span = x, jnp.zeros_like(x), 1
        while span < M:
            if span < per:
                lanes = span * dims
                rt = pltpu.roll(total, LANES - lanes, 1)
                t2 = shift(rt[:-SUB], rt[SUB:], lanes)
                if span > 1:
                    rd = pltpu.roll(dev, LANES - lanes, 1)
                    d2 = shift(rd[:-SUB], rd[SUB:], lanes)
                t1, d1 = total[:-SUB], dev[:-SUB]
            else:
                by = span // per * SUB
                t1, t2, d1, d2 = total[:-by], total[by:], dev[:-by], dev[by:]
            gap = t1 - t2
            more = gap * gap * (0.5 / span)
            dev = more if span == 1 else d1 + d2 + more
            total = t1 + t2
            span *= 2
        c_ref[...] = total[: chunk] * (1.0 / M)
        r_ref[...] = lax.rsqrt(dev[: chunk] * (1.0 / M) + epsilon) * ((M * dims) ** -0.5)

    def spread_lanes(v, b):
        lane = lax.broadcasted_iota(jnp.int32, v.shape, 1)
        return jnp.take_along_axis(v, lax.rem(lane, dims) + b * dims, axis=1)

    own_at = me * brows
    own_chunk = own_at // chunk
    in_chunk = own_at - own_chunk * chunk
    own_s = in_chunk // seg
    own_j = in_chunk - own_s * seg
    build(own_chunk * chunk)
    first = own_j * SUB + own_s
    c_own = c_ref[pl.ds(first, brows, stride=SUB), :]
    r_own = r_ref[pl.ds(first, brows, stride=SUB), :]
    for b in range(per):
        c_b, r_b = spread_lanes(c_own, b), spread_lanes(r_own, b)
        for m in range(steps):
            w = x_ref[b, pl.ds(first + m * SUB, brows, stride=SUB), :]
            own_ref[m, pl.ds(b, brows, stride=per), :] = (w - c_b) * r_b
    for m in range(steps):
        ownb_ref[:, m * LANES : (m + 1) * LANES] = own_ref[m].astype(jnp.bfloat16)

    exclusion = M // 4
    sub_i = lax.broadcasted_iota(jnp.int32, (SUB, rows), 0)
    lane_i = lax.broadcasted_iota(jnp.int32, (SUB, rows), 1)
    ahead = sub_i * (seg * per) - lane_i

    def sweep(base, carry):
        after, before = carry
        for b in range(per):
            slot = b % 2
            for j in range(0, seg, 2):
                at = j * SUB
                c_b = spread_lanes(c_ref[at : at + 2 * SUB, :], b)
                r_b = spread_lanes(r_ref[at : at + 2 * SUB, :], b)
                for m in range(steps):
                    w = x_ref[b, at + m * SUB : at + (m + 2) * SUB, :]
                    sc_ref[slot, at : at + 2 * SUB, m * LANES : (m + 1) * LANES] = (
                        (w - c_b) * r_b
                    ).astype(jnp.bfloat16)
            product = lax.dot_general(
                sc_ref[slot],
                ownb_ref[...],
                (((1,), (1,)), ((), ())),
                preferred_element_type=jnp.float32,
            )
            for j in range(seg):
                p = product[j * SUB : (j + 1) * SUB, :]
                off = (base + j) * per + b - me * rows
                after = jnp.maximum(after, jnp.where(ahead > exclusion - off, p, -1.0))
                before = jnp.maximum(before, jnp.where(ahead < -exclusion - off, p, -1.0))
        return after, before

    carry = (jnp.full((SUB, rows), -1.0, jnp.float32),) * 2
    if n_chunks == 1:
        carry = sweep(0, carry)
    else:

        def turn(i, carry):
            base = pl.multiple_of(i * chunk, chunk)
            build(base)
            return sweep(base, carry)

        carry = lax.fori_loop(0, n_chunks, turn, carry)
    after_ref[...] = 2.0 - 2.0 * jnp.max(carry[0], axis=0, keepdims=True)
    before_ref[...] = 2.0 - 2.0 * jnp.max(carry[1], axis=0, keepdims=True)


def profiles(start, pieces, masks, tail, rows, dims, n_blocks):
    per = LANES // dims
    brows = rows // per
    all_rows = n_blocks * brows
    chunk = min(256, all_rows)
    n_x = chunk + (M // per + 2) * SUB
    out = jax.ShapeDtypeStruct((1, rows), jnp.float32)
    vmem = pl.BlockSpec(memory_space=pltpu.VMEM)
    after, before = pl.pallas_call(
        functools.partial(profile_kernel, (masks, dims, rows, n_blocks)),
        out_shape=(out, out),
        in_specs=[pl.BlockSpec(memory_space=pltpu.SMEM)] + [vmem] * (len(pieces) + 1),
        out_specs=(vmem, vmem),
        scratch_shapes=[
            pltpu.VMEM((all_rows + tail.shape[0] + 2 * SUB, LANES), jnp.float32),
            pltpu.VMEM((per, n_x, LANES), jnp.float32),
            pltpu.VMEM((chunk, LANES), jnp.float32),
            pltpu.VMEM((chunk, LANES), jnp.float32),
            pltpu.VMEM((M // per, rows, LANES), jnp.float32),
            pltpu.VMEM((rows, M * dims), jnp.bfloat16),
            pltpu.VMEM((2, chunk, M * dims), jnp.bfloat16),
        ],
        name="profiles",
    )(start, *pieces, tail)
    return after.reshape(rows), before.reshape(rows)


def per_device(record, record_tail, projection, window_start):
    rows, dims = record.shape[0], projection.shape[1]
    n_blocks = lax.axis_size("pb") * lax.axis_size("row")
    p_t = projection.T
    mine = project(record, p_t)
    tail = project(record_tail, p_t)
    pieces, masks = [mine], [(0,)]
    held, held_masks = mine, (0,)
    for bit in reversed(range(n_blocks.bit_length() - 1)):
        got = lax.ppermute(held, AXES, [(i, i ^ (1 << bit)) for i in range(n_blocks)])
        got_masks = tuple(m ^ (1 << bit) for m in held_masks)
        pieces.append(got)
        masks.append(got_masks)
        held = jnp.concatenate([held, got], axis=0)
        held_masks = held_masks + got_masks
    return profiles(window_start, pieces, tuple(masks), tail, rows, dims, n_blocks)


def solution(mesh):
    return jax.shard_map(
        per_device,
        mesh=mesh,
        in_specs=(P(("grp", "pb", "row"), None), P("grp", None), P(), P("grp")),
        out_specs=(P(("grp", "pb", "row")), P(("grp", "pb", "row"))),
        check_vma=False,
    )
```

```python
import functools

import jax
import jax.numpy as jnp
from jax import lax
from jax.experimental import pallas as pl
from jax.experimental.pallas import tpu as pltpu
from jax.sharding import PartitionSpec as P

M = 64
LANES = 128
SUB = 8
epsilon = 1e-05
ceiling = 4.0
AXES = ("pb", "row")


def project_kernel(x_ref, p_ref, o_ref, y_ref):
    dims = p_ref.shape[0]
    per = LANES // dims
    rows = x_ref.shape[0]
    total = o_ref.shape[0] * per
    if rows != total:
        y_ref[...] = jnp.zeros_like(y_ref)
    y_ref[:rows, :] = lax.dot_general(
        x_ref[...],
        p_ref[...],
        (((1,), (1,)), ((), ())),
        precision=lax.Precision.HIGHEST,
        preferred_element_type=jnp.float32,
    )
    for u in range(per):
        o_ref[:, u * dims : (u + 1) * dims] = y_ref[pl.ds(u, total // per, stride=per), :]


def project(x, p_t):
    dims = p_t.shape[0]
    per = LANES // dims
    out_rows = -(-x.shape[0] // per)
    return pl.pallas_call(
        project_kernel,
        out_shape=pltpu.VMEM((out_rows, LANES), jnp.float32),
        in_specs=[pl.BlockSpec(memory_space=pltpu.VMEM)] * 2,
        out_specs=pl.BlockSpec(memory_space=pltpu.VMEM),
        scratch_shapes=[pltpu.VMEM((out_rows * per, dims), jnp.float32)],
        name="project",
    )(x, p_t)


def profile_kernel(cfg, start_ref, *refs):
    masks, dims, rows, n_blocks = cfg
    pieces = refs[: len(masks)]
    tail_ref, after_ref, before_ref = refs[len(masks) : len(masks) + 3]
    s_ref, x_ref, c_ref, r_ref, own_ref, ownb_ref, sc_ref = refs[len(masks) + 3 :]
    per = LANES // dims
    steps = M // per
    brows = rows // per
    all_rows = n_blocks * brows
    chunk = min(256, all_rows)
    seg = chunk // SUB
    n_chunks = all_rows // chunk
    n_x = (seg + steps + 2) * SUB
    me = lax.axis_index(AXES[0]) * lax.axis_size(AXES[1]) + lax.axis_index(AXES[1])

    for piece, piece_masks in zip(pieces, masks):
        for n, mask in enumerate(piece_masks):
            at = pl.multiple_of((me ^ mask) * brows, brows)
            s_ref[pl.ds(at, brows), :] = piece[n * brows : (n + 1) * brows, :]
    trows = tail_ref.shape[0]
    s_ref[all_rows : all_rows + trows, :] = tail_ref[...]
    pad = s_ref.shape[0] - all_rows - trows
    s_ref[all_rows + trows :, :] = jnp.zeros((pad, LANES), jnp.float32)

    start = start_ref[0]
    skip_rows = start // per
    skip = lax.rem(start, per) * dims

    def shift(first, second, lanes):
        lane = lax.broadcasted_iota(jnp.int32, first.shape, 1)
        return jnp.where(lane < LANES - lanes, first, second)

    def build(base):
        tiles = [
            s_ref[pl.ds(base + skip_rows + j, SUB, stride=seg), :] for j in range(seg + steps + 3)
        ]
        z = pltpu.roll(jnp.concatenate(tiles, axis=0), lax.rem(LANES - skip, LANES), 1)
        x = shift(z[:-SUB], z[SUB:], skip)
        x_ref[0] = x
        for b in range(1, per):
            y = pltpu.roll(x, LANES - b * dims, 1)
            x_ref[b, : n_x - SUB, :] = shift(y[:-SUB], y[SUB:], b * dims)
        total, dev, span = x, jnp.zeros_like(x), 1
        while span < M:
            if span < per:
                lanes = span * dims
                rt = pltpu.roll(total, LANES - lanes, 1)
                t2 = shift(rt[:-SUB], rt[SUB:], lanes)
                if span > 1:
                    rd = pltpu.roll(dev, LANES - lanes, 1)
                    d2 = shift(rd[:-SUB], rd[SUB:], lanes)
                t1, d1 = total[:-SUB], dev[:-SUB]
            else:
                by = span // per * SUB
                t1, t2, d1, d2 = total[:-by], total[by:], dev[:-by], dev[by:]
            gap = t1 - t2
            more = gap * gap * (0.5 / span)
            dev = more if span == 1 else d1 + d2 + more
            total = t1 + t2
            span *= 2
        c_ref[...] = total[: chunk] * (1.0 / M)
        r_ref[...] = lax.rsqrt(dev[: chunk] * (1.0 / M) + epsilon) * ((M * dims) ** -0.5)

    def spread_lanes(v, b):
        lane = lax.broadcasted_iota(jnp.int32, v.shape, 1)
        return jnp.take_along_axis(v, lax.rem(lane, dims) + b * dims, axis=1)

    own_at = me * brows
    own_chunk = own_at // chunk
    in_chunk = own_at - own_chunk * chunk
    own_s = in_chunk // seg
    own_j = in_chunk - own_s * seg
    build(own_chunk * chunk)
    first = own_j * SUB + own_s
    c_own = c_ref[pl.ds(first, brows, stride=SUB), :]
    r_own = r_ref[pl.ds(first, brows, stride=SUB), :]
    for b in range(per):
        c_b, r_b = spread_lanes(c_own, b), spread_lanes(r_own, b)
        for m in range(steps):
            w = x_ref[b, pl.ds(first + m * SUB, brows, stride=SUB), :]
            own_ref[m, pl.ds(b, brows, stride=per), :] = (w - c_b) * r_b
    for m in range(steps):
        ownb_ref[:, m * LANES : (m + 1) * LANES] = own_ref[m].astype(jnp.bfloat16)

    exclusion = M // 4
    sub_i = lax.broadcasted_iota(jnp.int32, (SUB, rows), 0)
    lane_i = lax.broadcasted_iota(jnp.int32, (SUB, rows), 1)
    ahead = sub_i * (seg * per) - lane_i

    def sweep(base, carry):
        after, before = carry
        for b in range(per):
            slot = b % 2
            for j in range(0, seg, 2):
                at = j * SUB
                c_b = spread_lanes(c_ref[at : at + 2 * SUB, :], b)
                r_b = spread_lanes(r_ref[at : at + 2 * SUB, :], b)
                for m in range(steps):
                    w = x_ref[b, at + m * SUB : at + (m + 2) * SUB, :]
                    sc_ref[slot, at : at + 2 * SUB, m * LANES : (m + 1) * LANES] = (
                        (w - c_b) * r_b
                    ).astype(jnp.bfloat16)
            product = lax.dot_general(
                sc_ref[slot],
                ownb_ref[...],
                (((1,), (1,)), ((), ())),
                preferred_element_type=jnp.float32,
            )
            for j in range(seg):
                p = product[j * SUB : (j + 1) * SUB, :]
                off = (base + j) * per + b - me * rows
                after = jnp.maximum(after, jnp.where(ahead > exclusion - off, p, -1.0))
                before = jnp.maximum(before, jnp.where(ahead < -exclusion - off, p, -1.0))
        return after, before

    carry = (jnp.full((SUB, rows), -1.0, jnp.float32),) * 2
    if n_chunks == 1:
        carry = sweep(0, carry)
    else:

        def turn(i, carry):
            base = pl.multiple_of(i * chunk, chunk)
            build(base)
            return sweep(base, carry)

        carry = lax.fori_loop(0, n_chunks, turn, carry)
    after_ref[...] = 2.0 - 2.0 * jnp.max(carry[0], axis=0, keepdims=True)
    before_ref[...] = 2.0 - 2.0 * jnp.max(carry[1], axis=0, keepdims=True)


def profiles(start, pieces, masks, tail, rows, dims, n_blocks):
    per = LANES // dims
    brows = rows // per
    all_rows = n_blocks * brows
    chunk = min(256, all_rows)
    n_x = chunk + (M // per + 2) * SUB
    out = jax.ShapeDtypeStruct((1, rows), jnp.float32)
    vmem = pl.BlockSpec(memory_space=pltpu.VMEM)
    after, before = pl.pallas_call(
        functools.partial(profile_kernel, (masks, dims, rows, n_blocks)),
        out_shape=(out, out),
        in_specs=[pl.BlockSpec(memory_space=pltpu.SMEM)] + [vmem] * (len(pieces) + 1),
        out_specs=(vmem, vmem),
        scratch_shapes=[
            pltpu.VMEM((all_rows + tail.shape[0] + 2 * SUB, LANES), jnp.float32),
            pltpu.VMEM((per, n_x, LANES), jnp.float32),
            pltpu.VMEM((chunk, LANES), jnp.float32),
            pltpu.VMEM((chunk, LANES), jnp.float32),
            pltpu.VMEM((M // per, rows, LANES), jnp.float32),
            pltpu.VMEM((rows, M * dims), jnp.bfloat16),
            pltpu.VMEM((2, chunk, M * dims), jnp.bfloat16),
        ],
        name="profiles",
    )(start, *[pltpu.with_memory_space_constraint(v, pltpu.VMEM) for v in (*pieces, tail)])
    return after.reshape(rows), before.reshape(rows)


def per_device(record, record_tail, projection, window_start):
    rows, dims = record.shape[0], projection.shape[1]
    n_blocks = lax.axis_size("pb") * lax.axis_size("row")
    p_t = projection.T
    mine = project(record, p_t)
    tail = project(record_tail, p_t)
    pieces, masks = [mine], [(0,)]
    held, held_masks = mine, (0,)
    for bit in reversed(range(n_blocks.bit_length() - 1)):
        got = lax.ppermute(held, AXES, [(i, i ^ (1 << bit)) for i in range(n_blocks)])
        got_masks = tuple(m ^ (1 << bit) for m in held_masks)
        if len(pieces) == 1:
            got, tail = lax.optimization_barrier((got, tail))
        pieces.append(got)
        masks.append(got_masks)
        held = jnp.concatenate([held, got], axis=0)
        held_masks = held_masks + got_masks
    return profiles(window_start, pieces, tuple(masks), tail, rows, dims, n_blocks)


def solution(mesh):
    return jax.shard_map(
        per_device,
        mesh=mesh,
        in_specs=(P(("grp", "pb", "row"), None), P("grp", None), P(), P("grp")),
        out_specs=(P(("grp", "pb", "row")), P(("grp", "pb", "row"))),
        check_vma=False,
    )
```

```python
import functools

import jax
import jax.numpy as jnp
from jax import lax
from jax.experimental import pallas as pl
from jax.experimental.pallas import tpu as pltpu
from jax.sharding import PartitionSpec as P

M = 64
LANES = 128
SUB = 8
epsilon = 1e-05
ceiling = 4.0
AXES = ("pb", "row")


def project_kernel(x_ref, p_ref, o_ref, y_ref):
    dims = p_ref.shape[0]
    per = LANES // dims
    rows = x_ref.shape[0]
    total = o_ref.shape[0] * per
    if rows != total:
        y_ref[...] = jnp.zeros_like(y_ref)
    y_ref[:rows, :] = lax.dot_general(
        x_ref[...],
        p_ref[...],
        (((1,), (1,)), ((), ())),
        precision=lax.Precision.HIGHEST,
        preferred_element_type=jnp.float32,
    )
    for u in range(per):
        o_ref[:, u * dims : (u + 1) * dims] = y_ref[pl.ds(u, total // per, stride=per), :]


def project(x, p_t):
    dims = p_t.shape[0]
    per = LANES // dims
    out_rows = -(-x.shape[0] // per)
    return pl.pallas_call(
        project_kernel,
        out_shape=pltpu.VMEM((out_rows, LANES), jnp.float32),
        in_specs=[pl.BlockSpec(memory_space=pltpu.VMEM)] * 2,
        out_specs=pl.BlockSpec(memory_space=pltpu.VMEM),
        scratch_shapes=[pltpu.VMEM((out_rows * per, dims), jnp.float32)],
        name="project",
    )(x, p_t)


def profile_kernel(cfg, start_ref, *refs):
    masks, dims, rows, n_blocks = cfg
    pieces = refs[: len(masks)]
    tail_ref, after_ref, before_ref = refs[len(masks) : len(masks) + 3]
    s_ref, x_ref, c_ref, r_ref, own_ref, xo_ref, yo_ref = refs[len(masks) + 3 :]
    per = LANES // dims
    steps = M // per
    brows = rows // per
    all_rows = n_blocks * brows
    chunk = min(256, all_rows)
    seg = chunk // SUB
    n_chunks = all_rows // chunk
    n_x = (seg + steps + 2) * SUB
    me = lax.axis_index(AXES[0]) * lax.axis_size(AXES[1]) + lax.axis_index(AXES[1])

    for piece, piece_masks in zip(pieces, masks):
        for n, mask in enumerate(piece_masks):
            at = pl.multiple_of((me ^ mask) * brows, brows)
            s_ref[pl.ds(at, brows), :] = piece[n * brows : (n + 1) * brows, :]
    trows = tail_ref.shape[0]
    s_ref[all_rows : all_rows + trows, :] = tail_ref[...]
    pad = s_ref.shape[0] - all_rows - trows
    s_ref[all_rows + trows :, :] = jnp.zeros((pad, LANES), jnp.float32)

    start = start_ref[0]
    skip_rows = start // per
    skip = lax.rem(start, per) * dims

    def shift(first, second, lanes):
        lane = lax.broadcasted_iota(jnp.int32, first.shape, 1)
        return jnp.where(lane < LANES - lanes, first, second)

    def build(base):
        tiles = [
            s_ref[pl.ds(base + skip_rows + j, SUB, stride=seg), :] for j in range(seg + steps + 3)
        ]
        z = pltpu.roll(jnp.concatenate(tiles, axis=0), lax.rem(LANES - skip, LANES), 1)
        x = shift(z[:-SUB], z[SUB:], skip)
        x_ref[0] = x
        total, dev, span = x, jnp.zeros_like(x), 1
        while span < M:
            if span < per:
                lanes = span * dims
                rt = pltpu.roll(total, LANES - lanes, 1)
                t2 = shift(rt[:-SUB], rt[SUB:], lanes)
                if span > 1:
                    rd = pltpu.roll(dev, LANES - lanes, 1)
                    d2 = shift(rd[:-SUB], rd[SUB:], lanes)
                t1, d1 = total[:-SUB], dev[:-SUB]
            else:
                by = span // per * SUB
                t1, t2, d1, d2 = total[:-by], total[by:], dev[:-by], dev[by:]
            gap = t1 - t2
            more = gap * gap * (0.5 / span)
            dev = more if span == 1 else d1 + d2 + more
            total = t1 + t2
            span *= 2
        c_ref[...] = total[: chunk] * (1.0 / M)
        r_ref[...] = lax.rsqrt(dev[: chunk] * (1.0 / M) + epsilon) * ((M * dims) ** -0.5)

    def spread_lanes(v, b):
        lane = lax.broadcasted_iota(jnp.int32, v.shape, 1)
        return jnp.take_along_axis(v, lax.rem(lane, dims) + b * dims, axis=1)

    own_at = me * brows
    own_chunk = own_at // chunk
    in_chunk = own_at - own_chunk * chunk
    own_s = in_chunk // seg
    own_j = in_chunk - own_s * seg
    n_own = brows + 2 * SUB
    take = own_at + skip_rows
    turn_by = lax.rem(LANES - skip, LANES)
    xo_ref[:n_own, :] = shift(
        pltpu.roll(s_ref[pl.ds(take, n_own), :], turn_by, 1),
        pltpu.roll(s_ref[pl.ds(take + 1, n_own), :], turn_by, 1),
        skip,
    )
    build(own_chunk * chunk)
    first = own_j * SUB + own_s
    c_own = c_ref[pl.ds(first, brows, stride=SUB), :]
    r_own = r_ref[pl.ds(first, brows, stride=SUB), :]
    for b in range(per):
        c_b, r_b = spread_lanes(c_own, b), spread_lanes(r_own, b)
        now = xo_ref[: n_own - SUB, :]
        if b:
            back = LANES - b * dims
            now = shift(pltpu.roll(now, back, 1), pltpu.roll(xo_ref[1 : n_own - SUB + 1, :], back, 1), b * dims)
        yo_ref[b] = now
        for m in range(steps):
            own_ref[m, pl.ds(b, brows, stride=per), :] = (yo_ref[b, m : m + brows, :] - c_b) * r_b
    own = jnp.concatenate([own_ref[m].astype(jnp.bfloat16) for m in range(steps)], axis=1)

    exclusion = M // 4
    sub_i = lax.broadcasted_iota(jnp.int32, (SUB, rows), 0)
    lane_i = lax.broadcasted_iota(jnp.int32, (SUB, rows), 1)
    ahead = sub_i * (seg * per) - lane_i

    def sweep(base, carry):
        after, before = carry
        for b in range(per):
            if b:
                y = pltpu.roll(x_ref[0], LANES - b * dims, 1)
                x_ref[b, : n_x - SUB, :] = shift(y[:-SUB], y[SUB:], b * dims)
            lines = []
            for j in range(0, seg, 2):
                at = j * SUB
                c_b = spread_lanes(c_ref[at : at + 2 * SUB, :], b)
                r_b = spread_lanes(r_ref[at : at + 2 * SUB, :], b)
                lines.append(
                    jnp.concatenate(
                        [
                            (
                                (x_ref[b, at + m * SUB : at + (m + 2) * SUB, :] - c_b) * r_b
                            ).astype(jnp.bfloat16)
                            for m in range(steps)
                        ],
                        axis=1,
                    )
                )
            product = lax.dot_general(
                jnp.concatenate(lines, axis=0),
                own,
                (((1,), (1,)), ((), ())),
                preferred_element_type=jnp.float32,
            )
            for j in range(seg):
                p = product[j * SUB : (j + 1) * SUB, :]
                off = (base + j) * per + b - me * rows
                after = jnp.maximum(after, jnp.where(ahead > exclusion - off, p, -1.0))
                before = jnp.maximum(before, jnp.where(ahead < -exclusion - off, p, -1.0))
        return after, before

    carry = (jnp.full((SUB, rows), -1.0, jnp.float32),) * 2
    if n_chunks == 1:
        carry = sweep(0, carry)
    else:

        def turn(i, carry):
            base = pl.multiple_of(i * chunk, chunk)
            build(base)
            return sweep(base, carry)

        carry = lax.fori_loop(0, n_chunks, turn, carry)
    after_ref[...] = 2.0 - 2.0 * jnp.max(carry[0], axis=0, keepdims=True)
    before_ref[...] = 2.0 - 2.0 * jnp.max(carry[1], axis=0, keepdims=True)


def profiles(start, pieces, masks, tail, rows, dims, n_blocks):
    per = LANES // dims
    brows = rows // per
    all_rows = n_blocks * brows
    chunk = min(256, all_rows)
    n_x = chunk + (M // per + 2) * SUB
    out = jax.ShapeDtypeStruct((1, rows), jnp.float32)
    vmem = pl.BlockSpec(memory_space=pltpu.VMEM)
    after, before = pl.pallas_call(
        functools.partial(profile_kernel, (masks, dims, rows, n_blocks)),
        out_shape=(out, out),
        in_specs=[pl.BlockSpec(memory_space=pltpu.SMEM)] + [vmem] * (len(pieces) + 1),
        out_specs=(vmem, vmem),
        scratch_shapes=[
            pltpu.VMEM((all_rows + tail.shape[0] + 2 * SUB, LANES), jnp.float32),
            pltpu.VMEM((per, n_x, LANES), jnp.float32),
            pltpu.VMEM((chunk, LANES), jnp.float32),
            pltpu.VMEM((chunk, LANES), jnp.float32),
            pltpu.VMEM((M // per, rows, LANES), jnp.float32),
            pltpu.VMEM((brows + 3 * SUB, LANES), jnp.float32),
            pltpu.VMEM((per, brows + SUB, LANES), jnp.float32),
        ],
        name="profiles",
    )(start, *[pltpu.with_memory_space_constraint(v, pltpu.VMEM) for v in (*pieces, tail)])
    return after.reshape(rows), before.reshape(rows)


def per_device(record, record_tail, projection, window_start):
    rows, dims = record.shape[0], projection.shape[1]
    n_blocks = lax.axis_size("pb") * lax.axis_size("row")
    p_t = projection.T
    mine = project(record, p_t)
    tail = project(record_tail, p_t)
    pieces, masks = [mine], [(0,)]
    held, held_masks = mine, (0,)
    for bit in reversed(range(n_blocks.bit_length() - 1)):
        got = lax.ppermute(held, AXES, [(i, i ^ (1 << bit)) for i in range(n_blocks)])
        got_masks = tuple(m ^ (1 << bit) for m in held_masks)
        if len(pieces) == 1:
            got, tail = lax.optimization_barrier((got, tail))
        pieces.append(got)
        masks.append(got_masks)
        held = jnp.concatenate([held, got], axis=0)
        held_masks = held_masks + got_masks
    return profiles(window_start, pieces, tuple(masks), tail, rows, dims, n_blocks)


def solution(mesh):
    return jax.shard_map(
        per_device,
        mesh=mesh,
        in_specs=(P(("grp", "pb", "row"), None), P("grp", None), P(), P("grp")),
        out_specs=(P(("grp", "pb", "row")), P(("grp", "pb", "row"))),
        check_vma=False,
    )
```

```python
import functools

import jax
import jax.numpy as jnp
from jax import lax
from jax.experimental import pallas as pl
from jax.experimental.pallas import tpu as pltpu
from jax.sharding import PartitionSpec as P

M = 64
LANES = 128
SUB = 8
epsilon = 1e-05
ceiling = 4.0
AXES = ("pb", "row")


def split3(v):
    hi = v.astype(jnp.bfloat16)
    rest = v - hi.astype(jnp.float32)
    mid = rest.astype(jnp.bfloat16)
    return hi, mid, (rest - mid.astype(jnp.float32)).astype(jnp.bfloat16)


def times_t(a, b):
    return lax.dot_general(a, b, (((1,), (1,)), ((), ())), preferred_element_type=jnp.float32)


def project_kernel(x_hbm, p_hbm, o_ref, x_ref, p_ref, y_ref, sems):
    dims = p_ref.shape[0]
    per = LANES // dims
    rows = x_ref.shape[0]
    total = o_ref.shape[0] * per
    load_p = pltpu.make_async_copy(p_hbm, p_ref, sems.at[1])
    load_x = pltpu.make_async_copy(x_hbm, x_ref, sems.at[0])
    load_p.start()
    load_x.start()
    if rows != total:
        y_ref[...] = jnp.zeros_like(y_ref)
    load_p.wait()
    parts = jnp.concatenate(split3(p_ref[...]), axis=0)
    load_x.wait()
    hi, mid, lo = [times_t(v, parts) for v in split3(x_ref[...])]
    low = lo[:, :dims] + mid[:, dims : 2 * dims] + hi[:, 2 * dims :]
    y_ref[:rows, :] = (low + (mid[:, :dims] + hi[:, dims : 2 * dims])) + hi[:, :dims]
    for u in range(per):
        o_ref[:, u * dims : (u + 1) * dims] = y_ref[pl.ds(u, total // per, stride=per), :]


def project(x, p_t):
    rows, width = x.shape
    dims = p_t.shape[0]
    per = LANES // dims
    out_rows = -(-rows // per)
    return pl.pallas_call(
        project_kernel,
        out_shape=pltpu.VMEM((out_rows, LANES), jnp.float32),
        in_specs=[pl.BlockSpec(memory_space=pl.ANY)] * 2,
        out_specs=pl.BlockSpec(memory_space=pltpu.VMEM),
        scratch_shapes=[
            pltpu.VMEM((rows, width), jnp.float32),
            pltpu.VMEM((dims, width), jnp.float32),
            pltpu.VMEM((out_rows * per, dims), jnp.float32),
            pltpu.SemaphoreType.DMA((2,)),
        ],
        name="project",
    )(x, p_t)


def profile_kernel(cfg, start_ref, *refs):
    masks, dims, rows, n_blocks = cfg
    pieces = refs[: len(masks)]
    tail_ref, after_ref, before_ref = refs[len(masks) : len(masks) + 3]
    s_ref, x_ref, c_ref, r_ref, own_ref, xo_ref, yo_ref = refs[len(masks) + 3 :]
    per = LANES // dims
    steps = M // per
    brows = rows // per
    all_rows = n_blocks * brows
    chunk = min(256, all_rows)
    seg = chunk // SUB
    n_chunks = all_rows // chunk
    n_x = (seg + steps + 2) * SUB
    me = lax.axis_index(AXES[0]) * lax.axis_size(AXES[1]) + lax.axis_index(AXES[1])

    for piece, piece_masks in zip(pieces, masks):
        for n, mask in enumerate(piece_masks):
            at = pl.multiple_of((me ^ mask) * brows, brows)
            s_ref[pl.ds(at, brows), :] = piece[n * brows : (n + 1) * brows, :]
    trows = tail_ref.shape[0]
    s_ref[all_rows : all_rows + trows, :] = tail_ref[...]
    pad = s_ref.shape[0] - all_rows - trows
    s_ref[all_rows + trows :, :] = jnp.zeros((pad, LANES), jnp.float32)

    start = start_ref[0]
    skip_rows = start // per
    skip = lax.rem(start, per) * dims

    def shift(first, second, lanes):
        lane = lax.broadcasted_iota(jnp.int32, first.shape, 1)
        return jnp.where(lane < LANES - lanes, first, second)

    def build(base):
        tiles = [
            s_ref[pl.ds(base + skip_rows + j, SUB, stride=seg), :] for j in range(seg + steps + 3)
        ]
        z = pltpu.roll(jnp.concatenate(tiles, axis=0), lax.rem(LANES - skip, LANES), 1)
        x = shift(z[:-SUB], z[SUB:], skip)
        x_ref[0] = x
        total, dev, span = x, jnp.zeros_like(x), 1
        while span < M:
            if span < per:
                lanes = span * dims
                rt = pltpu.roll(total, LANES - lanes, 1)
                t2 = shift(rt[:-SUB], rt[SUB:], lanes)
                if span > 1:
                    rd = pltpu.roll(dev, LANES - lanes, 1)
                    d2 = shift(rd[:-SUB], rd[SUB:], lanes)
                t1, d1 = total[:-SUB], dev[:-SUB]
            else:
                by = span // per * SUB
                t1, t2, d1, d2 = total[:-by], total[by:], dev[:-by], dev[by:]
            gap = t1 - t2
            more = gap * gap * (0.5 / span)
            dev = more if span == 1 else d1 + d2 + more
            total = t1 + t2
            span *= 2
        c_ref[...] = total[: chunk] * (1.0 / M)
        r_ref[...] = lax.rsqrt(dev[: chunk] * (1.0 / M) + epsilon) * ((M * dims) ** -0.5)

    def spread_lanes(v, b):
        lane = lax.broadcasted_iota(jnp.int32, v.shape, 1)
        return jnp.take_along_axis(v, lax.rem(lane, dims) + b * dims, axis=1)

    own_at = me * brows
    own_chunk = own_at // chunk
    in_chunk = own_at - own_chunk * chunk
    own_s = in_chunk // seg
    own_j = in_chunk - own_s * seg
    n_own = brows + 2 * SUB
    take = own_at + skip_rows
    turn_by = lax.rem(LANES - skip, LANES)
    xo_ref[:n_own, :] = shift(
        pltpu.roll(s_ref[pl.ds(take, n_own), :], turn_by, 1),
        pltpu.roll(s_ref[pl.ds(take + 1, n_own), :], turn_by, 1),
        skip,
    )
    build(own_chunk * chunk)
    first = own_j * SUB + own_s
    c_own = c_ref[pl.ds(first, brows, stride=SUB), :]
    r_own = r_ref[pl.ds(first, brows, stride=SUB), :]
    for b in range(per):
        c_b, r_b = spread_lanes(c_own, b), spread_lanes(r_own, b)
        now = xo_ref[: n_own - SUB, :]
        if b:
            back = LANES - b * dims
            now = shift(pltpu.roll(now, back, 1), pltpu.roll(xo_ref[1 : n_own - SUB + 1, :], back, 1), b * dims)
        yo_ref[b] = now
        for m in range(steps):
            own_ref[m, pl.ds(b, brows, stride=per), :] = (yo_ref[b, m : m + brows, :] - c_b) * r_b
    own = jnp.concatenate([own_ref[m].astype(jnp.bfloat16) for m in range(steps)], axis=1)

    exclusion = M // 4
    sub_i = lax.broadcasted_iota(jnp.int32, (SUB, rows), 0)
    lane_i = lax.broadcasted_iota(jnp.int32, (SUB, rows), 1)
    ahead = sub_i * (seg * per) - lane_i

    def sweep(base, carry):
        after, before = carry
        for b in range(per):
            if b:
                y = pltpu.roll(x_ref[0], LANES - b * dims, 1)
                x_ref[b, : n_x - SUB, :] = shift(y[:-SUB], y[SUB:], b * dims)
            lines = []
            for j in range(0, seg, 2):
                at = j * SUB
                c_b = spread_lanes(c_ref[at : at + 2 * SUB, :], b)
                r_b = spread_lanes(r_ref[at : at + 2 * SUB, :], b)
                lines.append(
                    jnp.concatenate(
                        [
                            (
                                (x_ref[b, at + m * SUB : at + (m + 2) * SUB, :] - c_b) * r_b
                            ).astype(jnp.bfloat16)
                            for m in range(steps)
                        ],
                        axis=1,
                    )
                )
            product = lax.dot_general(
                jnp.concatenate(lines, axis=0),
                own,
                (((1,), (1,)), ((), ())),
                preferred_element_type=jnp.float32,
            )
            for j in range(seg):
                p = product[j * SUB : (j + 1) * SUB, :]
                off = (base + j) * per + b - me * rows
                after = jnp.maximum(after, jnp.where(ahead > exclusion - off, p, -1.0))
                before = jnp.maximum(before, jnp.where(ahead < -exclusion - off, p, -1.0))
        return after, before

    carry = (jnp.full((SUB, rows), -1.0, jnp.float32),) * 2
    if n_chunks == 1:
        carry = sweep(0, carry)
    else:

        def turn(i, carry):
            base = pl.multiple_of(i * chunk, chunk)
            build(base)
            return sweep(base, carry)

        carry = lax.fori_loop(0, n_chunks, turn, carry)
    after_ref[...] = 2.0 - 2.0 * jnp.max(carry[0], axis=0, keepdims=True)
    before_ref[...] = 2.0 - 2.0 * jnp.max(carry[1], axis=0, keepdims=True)


def profiles(start, pieces, masks, tail, rows, dims, n_blocks):
    per = LANES // dims
    brows = rows // per
    all_rows = n_blocks * brows
    chunk = min(256, all_rows)
    n_x = chunk + (M // per + 2) * SUB
    out = jax.ShapeDtypeStruct((1, rows), jnp.float32)
    vmem = pl.BlockSpec(memory_space=pltpu.VMEM)
    after, before = pl.pallas_call(
        functools.partial(profile_kernel, (masks, dims, rows, n_blocks)),
        out_shape=(out, out),
        in_specs=[pl.BlockSpec(memory_space=pltpu.SMEM)] + [vmem] * (len(pieces) + 1),
        out_specs=(vmem, vmem),
        scratch_shapes=[
            pltpu.VMEM((all_rows + tail.shape[0] + 2 * SUB, LANES), jnp.float32),
            pltpu.VMEM((per, n_x, LANES), jnp.float32),
            pltpu.VMEM((chunk, LANES), jnp.float32),
            pltpu.VMEM((chunk, LANES), jnp.float32),
            pltpu.VMEM((M // per, rows, LANES), jnp.float32),
            pltpu.VMEM((brows + 3 * SUB, LANES), jnp.float32),
            pltpu.VMEM((per, brows + SUB, LANES), jnp.float32),
        ],
        name="profiles",
    )(start, *[pltpu.with_memory_space_constraint(v, pltpu.VMEM) for v in (*pieces, tail)])
    return after.reshape(rows), before.reshape(rows)


def per_device(record, record_tail, projection, window_start):
    rows, dims = record.shape[0], projection.shape[1]
    n_blocks = lax.axis_size("pb") * lax.axis_size("row")
    p_t = projection.T
    mine = project(record, p_t)
    tail = project(record_tail, p_t)
    bits = n_blocks.bit_length() - 1
    rounds = [(bit,) for bit in reversed(range(bits))]
    pieces, masks = [mine], [(0,)]
    held, held_masks = mine, (0,)
    for n, group in enumerate(rounds):
        news, new_masks = [], []
        for pick in range(1, 1 << len(group)):
            flip = sum(1 << bit for m, bit in enumerate(group) if pick >> m & 1)
            news.append(lax.ppermute(held, AXES, [(i, i ^ flip) for i in range(n_blocks)]))
            new_masks.append(tuple(m ^ flip for m in held_masks))
        if n == 0:
            *news, tail = lax.optimization_barrier((*news, tail))
        pieces += news
        masks += new_masks
        if n < len(rounds) - 1:
            held = jnp.concatenate([held, *news], axis=0)
            held_masks = held_masks + sum(new_masks, ())
    return profiles(window_start, pieces, tuple(masks), tail, rows, dims, n_blocks)


def solution(mesh):
    return jax.shard_map(
        per_device,
        mesh=mesh,
        in_specs=(P(("grp", "pb", "row"), None), P("grp", None), P(), P("grp")),
        out_specs=(P(("grp", "pb", "row")), P(("grp", "pb", "row"))),
        check_vma=False,
    )
```

```python
import functools

import jax
import jax.numpy as jnp
from jax import lax
from jax.experimental import pallas as pl
from jax.experimental.pallas import tpu as pltpu
from jax.sharding import PartitionSpec as P

M = 64
LANES = 128
SUB = 8
epsilon = 1e-05
ceiling = 4.0
AXES = ("pb", "row")


def split3(v):
    hi = v.astype(jnp.bfloat16)
    rest = v - hi.astype(jnp.float32)
    mid = rest.astype(jnp.bfloat16)
    return hi, mid, (rest - mid.astype(jnp.float32)).astype(jnp.bfloat16)


def times_t(a, b):
    return lax.dot_general(a, b, (((1,), (1,)), ((), ())), preferred_element_type=jnp.float32)


def project_rows(x_ref, parts, o_ref, y_ref):
    rows, dims = x_ref.shape[0], y_ref.shape[1]
    per = LANES // dims
    total = y_ref.shape[0]
    hi, mid, lo = [times_t(v, parts) for v in split3(x_ref[...])]
    low = lo[:, :dims] + mid[:, dims : 2 * dims] + hi[:, 2 * dims :]
    y_ref[:rows, :] = (low + (mid[:, :dims] + hi[:, dims : 2 * dims])) + hi[:, :dims]
    for u in range(per):
        o_ref[:, u * dims : (u + 1) * dims] = y_ref[pl.ds(u, total // per, stride=per), :]


def project_kernel(x_hbm, p_hbm, o_ref, parts_ref, x_ref, p_ref, y_ref, sems):
    load_p = pltpu.make_async_copy(p_hbm, p_ref, sems.at[1])
    load_x = pltpu.make_async_copy(x_hbm, x_ref, sems.at[0])
    load_p.start()
    load_x.start()
    if x_ref.shape[0] != y_ref.shape[0]:
        y_ref[...] = jnp.zeros_like(y_ref)
    load_p.wait()
    parts = jnp.concatenate(split3(p_ref[...]), axis=0)
    parts_ref[...] = parts
    load_x.wait()
    project_rows(x_ref, parts, o_ref, y_ref)


def project(x, p_t):
    rows, width = x.shape
    dims = p_t.shape[0]
    out_rows = -(-rows * dims // LANES)
    return pl.pallas_call(
        project_kernel,
        out_shape=(
            pltpu.VMEM((out_rows, LANES), jnp.float32),
            pltpu.VMEM((3 * dims, width), jnp.bfloat16),
        ),
        in_specs=[pl.BlockSpec(memory_space=pl.ANY)] * 2,
        out_specs=(pl.BlockSpec(memory_space=pltpu.VMEM),) * 2,
        scratch_shapes=[
            pltpu.VMEM((rows, width), jnp.float32),
            pltpu.VMEM((dims, width), jnp.float32),
            pltpu.VMEM((out_rows * (LANES // dims), dims), jnp.float32),
            pltpu.SemaphoreType.DMA((2,)),
        ],
        name="project",
    )(x, p_t)


def project_loaded_kernel(x_ref, parts_ref, o_ref, y_ref):
    if x_ref.shape[0] != y_ref.shape[0]:
        y_ref[...] = jnp.zeros_like(y_ref)
    project_rows(x_ref, parts_ref[...], o_ref, y_ref)


def project_loaded(x, parts):
    rows = x.shape[0]
    dims = parts.shape[0] // 3
    out_rows = -(-rows * dims // LANES)
    return pl.pallas_call(
        project_loaded_kernel,
        out_shape=pltpu.VMEM((out_rows, LANES), jnp.float32),
        in_specs=[pl.BlockSpec(memory_space=pltpu.VMEM)] * 2,
        out_specs=pl.BlockSpec(memory_space=pltpu.VMEM),
        scratch_shapes=[pltpu.VMEM((out_rows * (LANES // dims), dims), jnp.float32)],
        name="project_tail",
    )(*[pltpu.with_memory_space_constraint(v, pltpu.VMEM) for v in (x, parts)])


def profile_kernel(cfg, start_ref, *refs):
    masks, dims, rows, n_blocks = cfg
    pieces = refs[: len(masks)]
    tail_ref, after_ref, before_ref = refs[len(masks) : len(masks) + 3]
    s_ref, x_ref, c_ref, r_ref, own_ref, xo_ref, yo_ref = refs[len(masks) + 3 :]
    per = LANES // dims
    steps = M // per
    brows = rows // per
    all_rows = n_blocks * brows
    chunk = min(256, all_rows)
    seg = chunk // SUB
    n_chunks = all_rows // chunk
    n_x = (seg + steps + 2) * SUB
    me = lax.axis_index(AXES[0]) * lax.axis_size(AXES[1]) + lax.axis_index(AXES[1])

    for piece, piece_masks in zip(pieces, masks):
        for n, mask in enumerate(piece_masks):
            at = pl.multiple_of((me ^ mask) * brows, brows)
            s_ref[pl.ds(at, brows), :] = piece[n * brows : (n + 1) * brows, :]
    trows = tail_ref.shape[0]
    s_ref[all_rows : all_rows + trows, :] = tail_ref[...]
    pad = s_ref.shape[0] - all_rows - trows
    s_ref[all_rows + trows :, :] = jnp.zeros((pad, LANES), jnp.float32)

    start = start_ref[0]
    skip_rows = start // per
    skip = lax.rem(start, per) * dims

    def shift(first, second, lanes):
        lane = lax.broadcasted_iota(jnp.int32, first.shape, 1)
        return jnp.where(lane < LANES - lanes, first, second)

    def build(base):
        tiles = [
            s_ref[pl.ds(base + skip_rows + j, SUB, stride=seg), :] for j in range(seg + steps + 3)
        ]
        z = pltpu.roll(jnp.concatenate(tiles, axis=0), lax.rem(LANES - skip, LANES), 1)
        x = shift(z[:-SUB], z[SUB:], skip)
        x_ref[0] = x
        total, dev, span = x, jnp.zeros_like(x), 1
        while span < M:
            if span < per:
                lanes = span * dims
                rt = pltpu.roll(total, LANES - lanes, 1)
                t2 = shift(rt[:-SUB], rt[SUB:], lanes)
                if span > 1:
                    rd = pltpu.roll(dev, LANES - lanes, 1)
                    d2 = shift(rd[:-SUB], rd[SUB:], lanes)
                t1, d1 = total[:-SUB], dev[:-SUB]
            else:
                by = span // per * SUB
                t1, t2, d1, d2 = total[:-by], total[by:], dev[:-by], dev[by:]
            gap = t1 - t2
            more = gap * gap * (0.5 / span)
            dev = more if span == 1 else d1 + d2 + more
            total = t1 + t2
            span *= 2
        c_ref[...] = total[: chunk] * (1.0 / M)
        r_ref[...] = lax.rsqrt(dev[: chunk] * (1.0 / M) + epsilon) * ((M * dims) ** -0.5)

    def spread_lanes(v, b):
        lane = lax.broadcasted_iota(jnp.int32, v.shape, 1)
        return jnp.take_along_axis(v, lax.rem(lane, dims) + b * dims, axis=1)

    own_at = me * brows
    own_chunk = own_at // chunk
    in_chunk = own_at - own_chunk * chunk
    own_s = in_chunk // seg
    own_j = in_chunk - own_s * seg
    n_own = brows + 2 * SUB
    take = own_at + skip_rows
    turn_by = lax.rem(LANES - skip, LANES)
    xo_ref[:n_own, :] = shift(
        pltpu.roll(s_ref[pl.ds(take, n_own), :], turn_by, 1),
        pltpu.roll(s_ref[pl.ds(take + 1, n_own), :], turn_by, 1),
        skip,
    )
    build(own_chunk * chunk)
    first = own_j * SUB + own_s
    c_own = c_ref[pl.ds(first, brows, stride=SUB), :]
    r_own = r_ref[pl.ds(first, brows, stride=SUB), :]
    for b in range(per):
        c_b, r_b = spread_lanes(c_own, b), spread_lanes(r_own, b)
        now = xo_ref[: n_own - SUB, :]
        if b:
            back = LANES - b * dims
            now = shift(pltpu.roll(now, back, 1), pltpu.roll(xo_ref[1 : n_own - SUB + 1, :], back, 1), b * dims)
        yo_ref[b] = now
        for m in range(steps):
            own_ref[m, pl.ds(b, brows, stride=per), :] = (yo_ref[b, m : m + brows, :] - c_b) * r_b
    own = jnp.concatenate([own_ref[m].astype(jnp.bfloat16) for m in range(steps)], axis=1)

    exclusion = M // 4
    sub_i = lax.broadcasted_iota(jnp.int32, (SUB, rows), 0)
    lane_i = lax.broadcasted_iota(jnp.int32, (SUB, rows), 1)
    ahead = sub_i * (seg * per) - lane_i

    def sweep(base, carry):
        after, before = carry
        for b in range(per):
            if b:
                y = pltpu.roll(x_ref[0], LANES - b * dims, 1)
                x_ref[b, : n_x - SUB, :] = shift(y[:-SUB], y[SUB:], b * dims)
            lines = []
            for j in range(0, seg, 2):
                at = j * SUB
                c_b = spread_lanes(c_ref[at : at + 2 * SUB, :], b)
                r_b = spread_lanes(r_ref[at : at + 2 * SUB, :], b)
                lines.append(
                    jnp.concatenate(
                        [
                            (
                                (x_ref[b, at + m * SUB : at + (m + 2) * SUB, :] - c_b) * r_b
                            ).astype(jnp.bfloat16)
                            for m in range(steps)
                        ],
                        axis=1,
                    )
                )
            product = lax.dot_general(
                jnp.concatenate(lines, axis=0),
                own,
                (((1,), (1,)), ((), ())),
                preferred_element_type=jnp.float32,
            )
            for j in range(seg):
                p = product[j * SUB : (j + 1) * SUB, :]
                off = (base + j) * per + b - me * rows
                after = jnp.maximum(after, jnp.where(ahead > exclusion - off, p, -1.0))
                before = jnp.maximum(before, jnp.where(ahead < -exclusion - off, p, -1.0))
        return after, before

    carry = (jnp.full((SUB, rows), -1.0, jnp.float32),) * 2
    if n_chunks == 1:
        carry = sweep(0, carry)
    else:

        def turn(i, carry):
            base = pl.multiple_of(i * chunk, chunk)
            build(base)
            return sweep(base, carry)

        carry = lax.fori_loop(0, n_chunks, turn, carry)
    after_ref[...] = 2.0 - 2.0 * jnp.max(carry[0], axis=0, keepdims=True)
    before_ref[...] = 2.0 - 2.0 * jnp.max(carry[1], axis=0, keepdims=True)


def profiles(start, pieces, masks, tail, rows, dims, n_blocks):
    per = LANES // dims
    brows = rows // per
    all_rows = n_blocks * brows
    chunk = min(256, all_rows)
    n_x = chunk + (M // per + 2) * SUB
    out = jax.ShapeDtypeStruct((1, rows), jnp.float32)
    vmem = pl.BlockSpec(memory_space=pltpu.VMEM)
    after, before = pl.pallas_call(
        functools.partial(profile_kernel, (masks, dims, rows, n_blocks)),
        out_shape=(out, out),
        in_specs=[pl.BlockSpec(memory_space=pltpu.SMEM)] + [vmem] * (len(pieces) + 1),
        out_specs=(vmem, vmem),
        scratch_shapes=[
            pltpu.VMEM((all_rows + tail.shape[0] + 2 * SUB, LANES), jnp.float32),
            pltpu.VMEM((per, n_x, LANES), jnp.float32),
            pltpu.VMEM((chunk, LANES), jnp.float32),
            pltpu.VMEM((chunk, LANES), jnp.float32),
            pltpu.VMEM((M // per, rows, LANES), jnp.float32),
            pltpu.VMEM((brows + 3 * SUB, LANES), jnp.float32),
            pltpu.VMEM((per, brows + SUB, LANES), jnp.float32),
        ],
        name="profiles",
    )(start, *[pltpu.with_memory_space_constraint(v, pltpu.VMEM) for v in (*pieces, tail)])
    return after.reshape(rows), before.reshape(rows)


def per_device(record, record_tail, projection, window_start):
    rows, dims = record.shape[0], projection.shape[1]
    n_blocks = lax.axis_size("pb") * lax.axis_size("row")
    p_t = projection.T
    mine, parts = project(record, p_t)
    tail = project_loaded(record_tail, parts)
    bits = n_blocks.bit_length() - 1
    flips = [1 << bit | 1 for bit in reversed(range(1, bits))] + [1]
    pieces, masks = [mine], [(0,)]
    held, held_masks = mine, (0,)
    for flip in flips:
        got = lax.ppermute(held, AXES, [(i, i ^ flip) for i in range(n_blocks)])
        got_masks = tuple(m ^ flip for m in held_masks)
        if len(pieces) == 1:
            got, tail = lax.optimization_barrier((got, tail))
        pieces.append(got)
        masks.append(got_masks)
        if flip != flips[-1]:
            held = jnp.concatenate([held, got], axis=0)
            held_masks = held_masks + got_masks
    return profiles(window_start, pieces, tuple(masks), tail, rows, dims, n_blocks)


def solution(mesh):
    return jax.shard_map(
        per_device,
        mesh=mesh,
        in_specs=(P(("grp", "pb", "row"), None), P("grp", None), P(), P("grp")),
        out_specs=(P(("grp", "pb", "row")), P(("grp", "pb", "row"))),
        check_vma=False,
    )
```

```python
import functools

import jax
import jax.numpy as jnp
from jax import lax
from jax.experimental import pallas as pl
from jax.experimental.pallas import tpu as pltpu
from jax.sharding import PartitionSpec as P

M = 64
LANES = 128
SUB = 8
epsilon = 1e-05
ceiling = 4.0
AXES = ("pb", "row")


def split3(v):
    hi = v.astype(jnp.bfloat16)
    rest = v - hi.astype(jnp.float32)
    mid = rest.astype(jnp.bfloat16)
    return hi, mid, (rest - mid.astype(jnp.float32)).astype(jnp.bfloat16)


def times_t(a, b):
    return lax.dot_general(a, b, (((1,), (1,)), ((), ())), preferred_element_type=jnp.float32)


def project_rows(x_ref, parts, o_ref, y_ref):
    rows, dims = x_ref.shape[0], y_ref.shape[1]
    per = LANES // dims
    total = y_ref.shape[0]
    hi, mid, lo = [times_t(v, parts) for v in split3(x_ref[...])]
    low = lo[:, :dims] + mid[:, dims : 2 * dims] + hi[:, 2 * dims :]
    y_ref[:rows, :] = (low + (mid[:, :dims] + hi[:, dims : 2 * dims])) + hi[:, :dims]
    for u in range(per):
        o_ref[:, u * dims : (u + 1) * dims] = y_ref[pl.ds(u, total // per, stride=per), :]


def project_kernel(x_hbm, p_hbm, o_ref, parts_ref, x_ref, p_ref, y_ref, sems):
    load_p = pltpu.make_async_copy(p_hbm, p_ref, sems.at[1])
    load_x = pltpu.make_async_copy(x_hbm, x_ref, sems.at[0])
    load_p.start()
    load_x.start()
    if x_ref.shape[0] != y_ref.shape[0]:
        y_ref[...] = jnp.zeros_like(y_ref)
    load_p.wait()
    parts = jnp.concatenate(split3(p_ref[...]), axis=0)
    parts_ref[...] = parts
    load_x.wait()
    project_rows(x_ref, parts, o_ref, y_ref)


def project(x, p_t):
    rows, width = x.shape
    dims = p_t.shape[0]
    out_rows = -(-rows * dims // LANES)
    return pl.pallas_call(
        project_kernel,
        out_shape=(
            pltpu.VMEM((out_rows, LANES), jnp.float32),
            pltpu.VMEM((3 * dims, width), jnp.bfloat16),
        ),
        in_specs=[pl.BlockSpec(memory_space=pl.ANY)] * 2,
        out_specs=(pl.BlockSpec(memory_space=pltpu.VMEM),) * 2,
        scratch_shapes=[
            pltpu.VMEM((rows, width), jnp.float32),
            pltpu.VMEM((dims, width), jnp.float32),
            pltpu.VMEM((out_rows * (LANES // dims), dims), jnp.float32),
            pltpu.SemaphoreType.DMA((2,)),
        ],
        name="project",
    )(x, p_t)


def project_loaded_kernel(start_in, x_ref, parts_ref, o_ref, start_out, y_ref):
    start_out[0] = start_in[0]
    if x_ref.shape[0] != y_ref.shape[0]:
        y_ref[...] = jnp.zeros_like(y_ref)
    project_rows(x_ref, parts_ref[...], o_ref, y_ref)


def project_loaded(x, parts, start):
    rows = x.shape[0]
    dims = parts.shape[0] // 3
    out_rows = -(-rows * dims // LANES)
    return pl.pallas_call(
        project_loaded_kernel,
        out_shape=(pltpu.VMEM((out_rows, LANES), jnp.float32), pltpu.SMEM((1,), jnp.int32)),
        in_specs=[pl.BlockSpec(memory_space=pltpu.SMEM)]
        + [pl.BlockSpec(memory_space=pltpu.VMEM)] * 2,
        out_specs=(
            pl.BlockSpec(memory_space=pltpu.VMEM),
            pl.BlockSpec(memory_space=pltpu.SMEM),
        ),
        scratch_shapes=[pltpu.VMEM((out_rows * (LANES // dims), dims), jnp.float32)],
        name="project_tail",
    )(start, *[pltpu.with_memory_space_constraint(v, pltpu.VMEM) for v in (x, parts)])


def profile_kernel(cfg, start_ref, *refs):
    masks, dims, rows, n_blocks = cfg
    pieces = refs[: len(masks)]
    tail_ref, after_ref, before_ref = refs[len(masks) : len(masks) + 3]
    s_ref, x_ref, c_ref, r_ref, own_ref, xo_ref, yo_ref = refs[len(masks) + 3 :]
    per = LANES // dims
    steps = M // per
    brows = rows // per
    all_rows = n_blocks * brows
    chunk = min(256, all_rows)
    seg = chunk // SUB
    n_chunks = all_rows // chunk
    n_x = (seg + steps + 2) * SUB
    me = lax.axis_index(AXES[0]) * lax.axis_size(AXES[1]) + lax.axis_index(AXES[1])

    for piece, piece_masks in zip(pieces, masks):
        for n, mask in enumerate(piece_masks):
            at = pl.multiple_of((me ^ mask) * brows, brows)
            s_ref[pl.ds(at, brows), :] = piece[n * brows : (n + 1) * brows, :]
    trows = tail_ref.shape[0]
    s_ref[all_rows : all_rows + trows, :] = tail_ref[...]
    pad = s_ref.shape[0] - all_rows - trows
    s_ref[all_rows + trows :, :] = jnp.zeros((pad, LANES), jnp.float32)

    start = start_ref[0]
    skip_rows = start // per
    skip = lax.rem(start, per) * dims

    def shift(first, second, lanes):
        lane = lax.broadcasted_iota(jnp.int32, first.shape, 1)
        return jnp.where(lane < LANES - lanes, first, second)

    def build(base):
        tiles = [
            s_ref[pl.ds(base + skip_rows + j, SUB, stride=seg), :] for j in range(seg + steps + 3)
        ]
        z = pltpu.roll(jnp.concatenate(tiles, axis=0), lax.rem(LANES - skip, LANES), 1)
        x = shift(z[:-SUB], z[SUB:], skip)
        x_ref[0] = x
        total, dev, span = x, jnp.zeros_like(x), 1
        while span < M:
            if span < per:
                lanes = span * dims
                rt = pltpu.roll(total, LANES - lanes, 1)
                t2 = shift(rt[:-SUB], rt[SUB:], lanes)
                if span > 1:
                    rd = pltpu.roll(dev, LANES - lanes, 1)
                    d2 = shift(rd[:-SUB], rd[SUB:], lanes)
                t1, d1 = total[:-SUB], dev[:-SUB]
            else:
                by = span // per * SUB
                t1, t2, d1, d2 = total[:-by], total[by:], dev[:-by], dev[by:]
            gap = t1 - t2
            more = gap * gap * (0.5 / span)
            dev = more if span == 1 else d1 + d2 + more
            total = t1 + t2
            span *= 2
        c_ref[...] = total[: chunk] * (1.0 / M)
        r_ref[...] = lax.rsqrt(dev[: chunk] * (1.0 / M) + epsilon) * ((M * dims) ** -0.5)

    def spread_lanes(v, b):
        lane = lax.broadcasted_iota(jnp.int32, v.shape, 1)
        return jnp.take_along_axis(v, lax.rem(lane, dims) + b * dims, axis=1)

    own_at = me * brows
    own_chunk = own_at // chunk
    in_chunk = own_at - own_chunk * chunk
    own_s = in_chunk // seg
    own_j = in_chunk - own_s * seg
    n_own = brows + 2 * SUB
    take = own_at + skip_rows
    turn_by = lax.rem(LANES - skip, LANES)
    xo_ref[:n_own, :] = shift(
        pltpu.roll(s_ref[pl.ds(take, n_own), :], turn_by, 1),
        pltpu.roll(s_ref[pl.ds(take + 1, n_own), :], turn_by, 1),
        skip,
    )
    build(own_chunk * chunk)
    first = own_j * SUB + own_s
    c_own = c_ref[pl.ds(first, brows, stride=SUB), :]
    r_own = r_ref[pl.ds(first, brows, stride=SUB), :]
    for b in range(per):
        c_b, r_b = spread_lanes(c_own, b), spread_lanes(r_own, b)
        now = xo_ref[: n_own - SUB, :]
        if b:
            back = LANES - b * dims
            now = shift(pltpu.roll(now, back, 1), pltpu.roll(xo_ref[1 : n_own - SUB + 1, :], back, 1), b * dims)
        yo_ref[b] = now
        for m in range(steps):
            own_ref[m, pl.ds(b, brows, stride=per), :] = (yo_ref[b, m : m + brows, :] - c_b) * r_b
    own = jnp.concatenate([own_ref[m].astype(jnp.bfloat16) for m in range(steps)], axis=1)

    exclusion = M // 4
    sub_i = lax.broadcasted_iota(jnp.int32, (SUB, rows), 0)
    lane_i = lax.broadcasted_iota(jnp.int32, (SUB, rows), 1)
    ahead = sub_i * (seg * per) - lane_i

    def sweep(base, carry):
        after, before = carry
        for b in range(per):
            if b:
                y = pltpu.roll(x_ref[0], LANES - b * dims, 1)
                x_ref[b, : n_x - SUB, :] = shift(y[:-SUB], y[SUB:], b * dims)
            lines = []
            for j in range(0, seg, 2):
                at = j * SUB
                c_b = spread_lanes(c_ref[at : at + 2 * SUB, :], b)
                r_b = spread_lanes(r_ref[at : at + 2 * SUB, :], b)
                lines.append(
                    jnp.concatenate(
                        [
                            (
                                (x_ref[b, at + m * SUB : at + (m + 2) * SUB, :] - c_b) * r_b
                            ).astype(jnp.bfloat16)
                            for m in range(steps)
                        ],
                        axis=1,
                    )
                )
            product = lax.dot_general(
                jnp.concatenate(lines, axis=0),
                own,
                (((1,), (1,)), ((), ())),
                preferred_element_type=jnp.float32,
            )
            for j in range(seg):
                p = product[j * SUB : (j + 1) * SUB, :]
                off = (base + j) * per + b - me * rows
                after = jnp.maximum(after, jnp.where(ahead > exclusion - off, p, -1.0))
                before = jnp.maximum(before, jnp.where(ahead < -exclusion - off, p, -1.0))
        return after, before

    carry = (jnp.full((SUB, rows), -1.0, jnp.float32),) * 2
    if n_chunks == 1:
        carry = sweep(0, carry)
    else:

        def turn(i, carry):
            base = pl.multiple_of(i * chunk, chunk)
            build(base)
            return sweep(base, carry)

        carry = lax.fori_loop(0, n_chunks, turn, carry)
    after_ref[...] = 2.0 - 2.0 * jnp.max(carry[0], axis=0, keepdims=True)
    before_ref[...] = 2.0 - 2.0 * jnp.max(carry[1], axis=0, keepdims=True)


def profiles(start, pieces, masks, tail, rows, dims, n_blocks):
    per = LANES // dims
    brows = rows // per
    all_rows = n_blocks * brows
    chunk = min(256, all_rows)
    n_x = chunk + (M // per + 2) * SUB
    out = jax.ShapeDtypeStruct((1, rows), jnp.float32)
    vmem = pl.BlockSpec(memory_space=pltpu.VMEM)
    after, before = pl.pallas_call(
        functools.partial(profile_kernel, (masks, dims, rows, n_blocks)),
        out_shape=(out, out),
        in_specs=[pl.BlockSpec(memory_space=pltpu.SMEM)] + [vmem] * (len(pieces) + 1),
        out_specs=(vmem, vmem),
        scratch_shapes=[
            pltpu.VMEM((all_rows + tail.shape[0] + 2 * SUB, LANES), jnp.float32),
            pltpu.VMEM((per, n_x, LANES), jnp.float32),
            pltpu.VMEM((chunk, LANES), jnp.float32),
            pltpu.VMEM((chunk, LANES), jnp.float32),
            pltpu.VMEM((M // per, rows, LANES), jnp.float32),
            pltpu.VMEM((brows + 3 * SUB, LANES), jnp.float32),
            pltpu.VMEM((per, brows + SUB, LANES), jnp.float32),
        ],
        name="profiles",
    )(
        pltpu.with_memory_space_constraint(start, pltpu.SMEM),
        *[pltpu.with_memory_space_constraint(v, pltpu.VMEM) for v in (*pieces, tail)],
    )
    return after.reshape(rows), before.reshape(rows)


def per_device(record, record_tail, projection, window_start):
    rows, dims = record.shape[0], projection.shape[1]
    n_blocks = lax.axis_size("pb") * lax.axis_size("row")
    p_t = projection.T
    mine, parts = project(record, p_t)
    tail, start = project_loaded(record_tail, parts, window_start)
    bits = n_blocks.bit_length() - 1
    flips = [1 << bit | 1 for bit in reversed(range(1, bits))] + [1]
    pieces, masks = [mine], [(0,)]
    held, held_masks = mine, (0,)
    for flip in flips:
        got = lax.ppermute(held, AXES, [(i, i ^ flip) for i in range(n_blocks)])
        got_masks = tuple(m ^ flip for m in held_masks)
        if len(pieces) == 1:
            got, tail = lax.optimization_barrier((got, tail))
        pieces.append(got)
        masks.append(got_masks)
        if flip != flips[-1]:
            held = jnp.concatenate([held, got], axis=0)
            held_masks = held_masks + got_masks
    return profiles(start, pieces, tuple(masks), tail, rows, dims, n_blocks)


def solution(mesh):
    return jax.shard_map(
        per_device,
        mesh=mesh,
        in_specs=(P(("grp", "pb", "row"), None), P("grp", None), P(), P("grp")),
        out_specs=(P(("grp", "pb", "row")), P(("grp", "pb", "row"))),
        check_vma=False,
    )
```

```python
import functools

import jax
import jax.numpy as jnp
from jax import lax
from jax.experimental import pallas as pl
from jax.experimental.pallas import tpu as pltpu
from jax.sharding import PartitionSpec as P

M = 64
LANES = 128
SUB = 8
epsilon = 1e-05
ceiling = 4.0
AXES = ("pb", "row")
SPLIT = 2


def split3(v):
    hi = v.astype(jnp.bfloat16)
    rest = v - hi.astype(jnp.float32)
    mid = rest.astype(jnp.bfloat16)
    return hi, mid, (rest - mid.astype(jnp.float32)).astype(jnp.bfloat16)


def times_t(a, b):
    return lax.dot_general(a, b, (((1,), (1,)), ((), ())), preferred_element_type=jnp.float32)


def project_rows(x_ref, parts, o_ref, y_ref):
    rows, dims = x_ref.shape[0], y_ref.shape[1]
    per = LANES // dims
    total = y_ref.shape[0]
    hi, mid, lo = [times_t(v, parts) for v in split3(x_ref[...])]
    low = lo[:, :dims] + mid[:, dims : 2 * dims] + hi[:, 2 * dims :]
    y_ref[:rows, :] = (low + (mid[:, :dims] + hi[:, dims : 2 * dims])) + hi[:, :dims]
    for u in range(per):
        o_ref[:, u * dims : (u + 1) * dims] = y_ref[pl.ds(u, total // per, stride=per), :]


def project_kernel(x_hbm, p_hbm, o_ref, parts_ref, x_ref, p_ref, y_ref, sems):
    load_p = pltpu.make_async_copy(p_hbm, p_ref, sems.at[1])
    load_x = pltpu.make_async_copy(x_hbm, x_ref, sems.at[0])
    load_p.start()
    load_x.start()
    if x_ref.shape[0] != y_ref.shape[0]:
        y_ref[...] = jnp.zeros_like(y_ref)
    load_p.wait()
    parts = jnp.concatenate(split3(p_ref[...]), axis=0)
    parts_ref[...] = parts
    load_x.wait()
    project_rows(x_ref, parts, o_ref, y_ref)


def project(x, p_t):
    rows, width = x.shape
    dims = p_t.shape[0]
    out_rows = -(-rows * dims // LANES)
    return pl.pallas_call(
        project_kernel,
        out_shape=(
            pltpu.VMEM((out_rows, LANES), jnp.float32),
            pltpu.VMEM((3 * dims, width), jnp.bfloat16),
        ),
        in_specs=[pl.BlockSpec(memory_space=pl.ANY)] * 2,
        out_specs=(pl.BlockSpec(memory_space=pltpu.VMEM),) * 2,
        scratch_shapes=[
            pltpu.VMEM((rows, width), jnp.float32),
            pltpu.VMEM((dims, width), jnp.float32),
            pltpu.VMEM((out_rows * (LANES // dims), dims), jnp.float32),
            pltpu.SemaphoreType.DMA((2,)),
        ],
        name="project",
    )(x, p_t)


def project_loaded_kernel(start_in, x_ref, parts_ref, o_ref, start_out, y_ref):
    start_out[0] = start_in[0]
    if x_ref.shape[0] != y_ref.shape[0]:
        y_ref[...] = jnp.zeros_like(y_ref)
    project_rows(x_ref, parts_ref[...], o_ref, y_ref)


def project_loaded(x, parts, start):
    rows = x.shape[0]
    dims = parts.shape[0] // 3
    out_rows = -(-rows * dims // LANES)
    return pl.pallas_call(
        project_loaded_kernel,
        out_shape=(pltpu.VMEM((out_rows, LANES), jnp.float32), pltpu.SMEM((1,), jnp.int32)),
        in_specs=[pl.BlockSpec(memory_space=pltpu.SMEM)]
        + [pl.BlockSpec(memory_space=pltpu.VMEM)] * 2,
        out_specs=(
            pl.BlockSpec(memory_space=pltpu.VMEM),
            pl.BlockSpec(memory_space=pltpu.SMEM),
        ),
        scratch_shapes=[pltpu.VMEM((out_rows * (LANES // dims), dims), jnp.float32)],
        name="project_tail",
    )(start, *[pltpu.with_memory_space_constraint(v, pltpu.VMEM) for v in (x, parts)])


def profile_kernel(cfg, start_ref, *refs):
    masks, dims, rows, n_blocks = cfg
    pieces = refs[: len(masks)]
    tail_ref, after_ref, before_ref = refs[len(masks) : len(masks) + 3]
    s_ref, x_ref, c_ref, r_ref, own_ref, xo_ref, yo_ref = refs[len(masks) + 3 :]
    per = LANES // dims
    steps = M // per
    brows = rows // per
    all_rows = n_blocks * brows
    chunk = min(256, all_rows)
    seg = chunk // SUB
    n_chunks = all_rows // chunk
    n_x = (seg + steps + 2) * SUB
    me = lax.axis_index(AXES[0]) * lax.axis_size(AXES[1]) + lax.axis_index(AXES[1])

    for piece, piece_masks in zip(pieces, masks):
        for n, mask in enumerate(piece_masks):
            at = pl.multiple_of((me ^ mask) * brows, brows)
            s_ref[pl.ds(at, brows), :] = piece[n * brows : (n + 1) * brows, :]
    trows = tail_ref.shape[0]
    s_ref[all_rows : all_rows + trows, :] = tail_ref[...]
    pad = s_ref.shape[0] - all_rows - trows
    s_ref[all_rows + trows :, :] = jnp.zeros((pad, LANES), jnp.float32)

    start = start_ref[0]
    skip_rows = start // per
    skip = lax.rem(start, per) * dims

    def shift(first, second, lanes):
        lane = lax.broadcasted_iota(jnp.int32, first.shape, 1)
        return jnp.where(lane < LANES - lanes, first, second)

    def build(base):
        tiles = [
            s_ref[pl.ds(base + skip_rows + j, SUB, stride=seg), :] for j in range(seg + steps + 3)
        ]
        z = pltpu.roll(jnp.concatenate(tiles, axis=0), lax.rem(LANES - skip, LANES), 1)
        x = shift(z[:-SUB], z[SUB:], skip)
        x_ref[0] = x
        total, dev, span = x, jnp.zeros_like(x), 1
        while span < M:
            if span < per:
                lanes = span * dims
                rt = pltpu.roll(total, LANES - lanes, 1)
                t2 = shift(rt[:-SUB], rt[SUB:], lanes)
                if span > 1:
                    rd = pltpu.roll(dev, LANES - lanes, 1)
                    d2 = shift(rd[:-SUB], rd[SUB:], lanes)
                t1, d1 = total[:-SUB], dev[:-SUB]
            else:
                by = span // per * SUB
                t1, t2, d1, d2 = total[:-by], total[by:], dev[:-by], dev[by:]
            gap = t1 - t2
            more = gap * gap * (0.5 / span)
            dev = more if span == 1 else d1 + d2 + more
            total = t1 + t2
            span *= 2
        c_ref[...] = total[: chunk] * (1.0 / M)
        r_ref[...] = lax.rsqrt(dev[: chunk] * (1.0 / M) + epsilon) * ((M * dims) ** -0.5)

    def spread_lanes(v, b):
        lane = lax.broadcasted_iota(jnp.int32, v.shape, 1)
        return jnp.take_along_axis(v, lax.rem(lane, dims) + b * dims, axis=1)

    own_at = me * brows
    own_chunk = own_at // chunk
    in_chunk = own_at - own_chunk * chunk
    own_s = in_chunk // seg
    own_j = in_chunk - own_s * seg
    n_own = brows + 2 * SUB
    take = own_at + skip_rows
    turn_by = lax.rem(LANES - skip, LANES)
    xo_ref[:n_own, :] = shift(
        pltpu.roll(s_ref[pl.ds(take, n_own), :], turn_by, 1),
        pltpu.roll(s_ref[pl.ds(take + 1, n_own), :], turn_by, 1),
        skip,
    )
    build(own_chunk * chunk)
    first = own_j * SUB + own_s
    c_own = c_ref[pl.ds(first, brows, stride=SUB), :]
    r_own = r_ref[pl.ds(first, brows, stride=SUB), :]
    for b in range(per):
        c_b, r_b = spread_lanes(c_own, b), spread_lanes(r_own, b)
        now = xo_ref[: n_own - SUB, :]
        if b:
            back = LANES - b * dims
            now = shift(pltpu.roll(now, back, 1), pltpu.roll(xo_ref[1 : n_own - SUB + 1, :], back, 1), b * dims)
        yo_ref[b] = now
        for m in range(steps):
            own_ref[m, pl.ds(b, brows, stride=per), :] = (yo_ref[b, m : m + brows, :] - c_b) * r_b
    own = jnp.concatenate([own_ref[m].astype(jnp.bfloat16) for m in range(steps)], axis=1)

    exclusion = M // 4
    sub_i = lax.broadcasted_iota(jnp.int32, (SUB, rows), 0)
    lane_i = lax.broadcasted_iota(jnp.int32, (SUB, rows), 1)
    ahead = sub_i * (seg * per) - lane_i

    def sweep(base, carry):
        after, before = carry
        some = seg // SPLIT
        for b in range(per):
            if b:
                y = pltpu.roll(x_ref[0], LANES - b * dims, 1)
                x_ref[b, : n_x - SUB, :] = shift(y[:-SUB], y[SUB:], b * dims)
            for part in range(0, seg, some):
                lines = []
                for j in range(part, part + some, 2):
                    at = j * SUB
                    c_b = spread_lanes(c_ref[at : at + 2 * SUB, :], b)
                    r_b = spread_lanes(r_ref[at : at + 2 * SUB, :], b)
                    lines.append(
                        jnp.concatenate(
                            [
                                (
                                    (x_ref[b, at + m * SUB : at + (m + 2) * SUB, :] - c_b) * r_b
                                ).astype(jnp.bfloat16)
                                for m in range(steps)
                            ],
                            axis=1,
                        )
                    )
                product = times_t(jnp.concatenate(lines, axis=0), own)
                for j in range(some):
                    p = product[j * SUB : (j + 1) * SUB, :]
                    off = (base + part + j) * per + b - me * rows
                    after = jnp.maximum(after, jnp.where(ahead > exclusion - off, p, -1.0))
                    before = jnp.maximum(before, jnp.where(ahead < -exclusion - off, p, -1.0))
        return after, before

    carry = (jnp.full((SUB, rows), -1.0, jnp.float32),) * 2
    if n_chunks == 1:
        carry = sweep(0, carry)
    else:

        def turn(i, carry):
            base = pl.multiple_of(i * chunk, chunk)
            build(base)
            return sweep(base, carry)

        carry = lax.fori_loop(0, n_chunks, turn, carry)
    after_ref[...] = 2.0 - 2.0 * jnp.max(carry[0], axis=0, keepdims=True)
    before_ref[...] = 2.0 - 2.0 * jnp.max(carry[1], axis=0, keepdims=True)


def profiles(start, pieces, masks, tail, rows, dims, n_blocks):
    per = LANES // dims
    brows = rows // per
    all_rows = n_blocks * brows
    chunk = min(256, all_rows)
    n_x = chunk + (M // per + 2) * SUB
    out = jax.ShapeDtypeStruct((1, rows), jnp.float32)
    vmem = pl.BlockSpec(memory_space=pltpu.VMEM)
    after, before = pl.pallas_call(
        functools.partial(profile_kernel, (masks, dims, rows, n_blocks)),
        out_shape=(out, out),
        in_specs=[pl.BlockSpec(memory_space=pltpu.SMEM)] + [vmem] * (len(pieces) + 1),
        out_specs=(vmem, vmem),
        scratch_shapes=[
            pltpu.VMEM((all_rows + tail.shape[0] + 2 * SUB, LANES), jnp.float32),
            pltpu.VMEM((per, n_x, LANES), jnp.float32),
            pltpu.VMEM((chunk, LANES), jnp.float32),
            pltpu.VMEM((chunk, LANES), jnp.float32),
            pltpu.VMEM((M // per, rows, LANES), jnp.float32),
            pltpu.VMEM((brows + 3 * SUB, LANES), jnp.float32),
            pltpu.VMEM((per, brows + SUB, LANES), jnp.float32),
        ],
        name="profiles",
    )(
        pltpu.with_memory_space_constraint(start, pltpu.SMEM),
        *[pltpu.with_memory_space_constraint(v, pltpu.VMEM) for v in (*pieces, tail)],
    )
    return after.reshape(rows), before.reshape(rows)


def per_device(record, record_tail, projection, window_start):
    rows, dims = record.shape[0], projection.shape[1]
    n_blocks = lax.axis_size("pb") * lax.axis_size("row")
    p_t = projection.T
    mine, parts = project(record, p_t)
    tail, start = project_loaded(record_tail, parts, window_start)
    bits = n_blocks.bit_length() - 1
    flips = [1 << bit | 1 for bit in reversed(range(1, bits))] + [1]
    pieces, masks = [mine], [(0,)]
    held, held_masks = mine, (0,)
    for flip in flips:
        got = lax.ppermute(held, AXES, [(i, i ^ flip) for i in range(n_blocks)])
        got_masks = tuple(m ^ flip for m in held_masks)
        if len(pieces) == 1:
            got, tail = lax.optimization_barrier((got, tail))
        pieces.append(got)
        masks.append(got_masks)
        if flip != flips[-1]:
            held = jnp.concatenate([held, got], axis=0)
            held_masks = held_masks + got_masks
    return profiles(start, pieces, tuple(masks), tail, rows, dims, n_blocks)


def solution(mesh):
    return jax.shard_map(
        per_device,
        mesh=mesh,
        in_specs=(P(("grp", "pb", "row"), None), P("grp", None), P(), P("grp")),
        out_specs=(P(("grp", "pb", "row")), P(("grp", "pb", "row"))),
        check_vma=False,
    )
```

```python
import functools

import jax
import jax.numpy as jnp
from jax import lax
from jax.experimental import pallas as pl
from jax.experimental.pallas import tpu as pltpu
from jax.sharding import PartitionSpec as P

M = 64
LANES = 128
SUB = 8
epsilon = 1e-05
ceiling = 4.0
AXES = ("pb", "row")
SPLIT = 2


def split3(v):
    hi = v.astype(jnp.bfloat16)
    rest = v - hi.astype(jnp.float32)
    mid = rest.astype(jnp.bfloat16)
    return hi, mid, (rest - mid.astype(jnp.float32)).astype(jnp.bfloat16)


def times_t(a, b):
    return lax.dot_general(a, b, (((1,), (1,)), ((), ())), preferred_element_type=jnp.float32)


def project_rows(x_ref, parts, o_ref, y_ref):
    rows, dims = x_ref.shape[0], y_ref.shape[1]
    per = LANES // dims
    total = y_ref.shape[0]
    hi, mid, lo = [times_t(v, parts) for v in split3(x_ref[...])]
    low = lo[:, :dims] + mid[:, dims : 2 * dims] + hi[:, 2 * dims :]
    y_ref[:rows, :] = (low + (mid[:, :dims] + hi[:, dims : 2 * dims])) + hi[:, :dims]
    for u in range(per):
        o_ref[:, u * dims : (u + 1) * dims] = y_ref[pl.ds(u, total // per, stride=per), :]


def project_kernel(x_hbm, p_hbm, o_ref, parts_ref, x_ref, p_ref, y_ref, sems):
    load_p = pltpu.make_async_copy(p_hbm, p_ref, sems.at[1])
    load_x = pltpu.make_async_copy(x_hbm, x_ref, sems.at[0])
    load_p.start()
    load_x.start()
    if x_ref.shape[0] != y_ref.shape[0]:
        y_ref[...] = jnp.zeros_like(y_ref)
    load_p.wait()
    parts = jnp.concatenate(split3(p_ref[...]), axis=0)
    parts_ref[...] = parts
    load_x.wait()
    project_rows(x_ref, parts, o_ref, y_ref)


def project(x, p_t):
    rows, width = x.shape
    dims = p_t.shape[0]
    out_rows = -(-rows * dims // LANES)
    return pl.pallas_call(
        project_kernel,
        out_shape=(
            pltpu.VMEM((out_rows, LANES), jnp.float32),
            pltpu.VMEM((3 * dims, width), jnp.bfloat16),
        ),
        in_specs=[pl.BlockSpec(memory_space=pl.ANY)] * 2,
        out_specs=(pl.BlockSpec(memory_space=pltpu.VMEM),) * 2,
        scratch_shapes=[
            pltpu.VMEM((rows, width), jnp.float32),
            pltpu.VMEM((dims, width), jnp.float32),
            pltpu.VMEM((out_rows * (LANES // dims), dims), jnp.float32),
            pltpu.SemaphoreType.DMA((2,)),
        ],
        name="project",
    )(x, p_t)


def project_loaded_kernel(start_in, x_ref, parts_ref, o_ref, start_out, y_ref):
    start_out[0] = start_in[0]
    if x_ref.shape[0] != y_ref.shape[0]:
        y_ref[...] = jnp.zeros_like(y_ref)
    project_rows(x_ref, parts_ref[...], o_ref, y_ref)


def project_loaded(x, parts, start):
    rows = x.shape[0]
    dims = parts.shape[0] // 3
    out_rows = -(-rows * dims // LANES)
    return pl.pallas_call(
        project_loaded_kernel,
        out_shape=(pltpu.VMEM((out_rows, LANES), jnp.float32), pltpu.SMEM((1,), jnp.int32)),
        in_specs=[pl.BlockSpec(memory_space=pltpu.SMEM)]
        + [pl.BlockSpec(memory_space=pltpu.VMEM)] * 2,
        out_specs=(
            pl.BlockSpec(memory_space=pltpu.VMEM),
            pl.BlockSpec(memory_space=pltpu.SMEM),
        ),
        scratch_shapes=[pltpu.VMEM((out_rows * (LANES // dims), dims), jnp.float32)],
        name="project_tail",
    )(start, *[pltpu.with_memory_space_constraint(v, pltpu.VMEM) for v in (x, parts)])


def profile_kernel(cfg, start_ref, *refs):
    masks, dims, rows, n_blocks = cfg
    pieces = refs[: len(masks)]
    tail_ref, after_ref, before_ref = refs[len(masks) : len(masks) + 3]
    s_ref, x_ref, c_ref, r_ref, xo_ref, yo_ref = refs[len(masks) + 3 :]
    per = LANES // dims
    steps = M // per
    brows = rows // per
    all_rows = n_blocks * brows
    chunk = min(256, all_rows)
    seg = chunk // SUB
    n_chunks = all_rows // chunk
    n_x = (seg + steps + 2) * SUB
    me = lax.axis_index(AXES[0]) * lax.axis_size(AXES[1]) + lax.axis_index(AXES[1])

    for piece, piece_masks in zip(pieces, masks):
        for n, mask in enumerate(piece_masks):
            at = pl.multiple_of((me ^ mask) * brows, brows)
            s_ref[pl.ds(at, brows), :] = piece[n * brows : (n + 1) * brows, :]
    trows = tail_ref.shape[0]
    s_ref[all_rows : all_rows + trows, :] = tail_ref[...]
    pad = s_ref.shape[0] - all_rows - trows
    s_ref[all_rows + trows :, :] = jnp.zeros((pad, LANES), jnp.float32)

    start = start_ref[0]
    skip_rows = start // per
    skip = lax.rem(start, per) * dims

    def shift(first, second, lanes):
        lane = lax.broadcasted_iota(jnp.int32, first.shape, 1)
        return jnp.where(lane < LANES - lanes, first, second)

    def build(base):
        tiles = [
            s_ref[pl.ds(base + skip_rows + j, SUB, stride=seg), :] for j in range(seg + steps + 3)
        ]
        z = pltpu.roll(jnp.concatenate(tiles, axis=0), lax.rem(LANES - skip, LANES), 1)
        x = shift(z[:-SUB], z[SUB:], skip)
        x_ref[0] = x
        total, dev, span = x, jnp.zeros_like(x), 1
        while span < M:
            if span < per:
                lanes = span * dims
                rt = pltpu.roll(total, LANES - lanes, 1)
                t2 = shift(rt[:-SUB], rt[SUB:], lanes)
                if span > 1:
                    rd = pltpu.roll(dev, LANES - lanes, 1)
                    d2 = shift(rd[:-SUB], rd[SUB:], lanes)
                t1, d1 = total[:-SUB], dev[:-SUB]
            else:
                by = span // per * SUB
                t1, t2, d1, d2 = total[:-by], total[by:], dev[:-by], dev[by:]
            gap = t1 - t2
            more = gap * gap * (0.5 / span)
            dev = more if span == 1 else d1 + d2 + more
            total = t1 + t2
            span *= 2
        c_ref[...] = total[: chunk] * (1.0 / M)
        r_ref[...] = lax.rsqrt(dev[: chunk] * (1.0 / M) + epsilon) * ((M * dims) ** -0.5)

    def spread_lanes(v, b):
        lane = lax.broadcasted_iota(jnp.int32, v.shape, 1)
        return jnp.take_along_axis(v, lax.rem(lane, dims) + b * dims, axis=1)

    own_at = me * brows
    own_chunk = own_at // chunk
    in_chunk = own_at - own_chunk * chunk
    own_s = in_chunk // seg
    own_j = in_chunk - own_s * seg
    n_own = brows + 2 * SUB
    take = own_at + skip_rows
    turn_by = lax.rem(LANES - skip, LANES)
    xo_ref[:n_own, :] = shift(
        pltpu.roll(s_ref[pl.ds(take, n_own), :], turn_by, 1),
        pltpu.roll(s_ref[pl.ds(take + 1, n_own), :], turn_by, 1),
        skip,
    )
    build(own_chunk * chunk)
    first = own_j * SUB + own_s
    c_own = c_ref[pl.ds(first, brows, stride=SUB), :]
    r_own = r_ref[pl.ds(first, brows, stride=SUB), :]
    lines = []
    for b in range(per):
        c_b, r_b = spread_lanes(c_own, b), spread_lanes(r_own, b)
        now = xo_ref[: n_own - SUB, :]
        if b:
            back = LANES - b * dims
            now = shift(pltpu.roll(now, back, 1), pltpu.roll(xo_ref[1 : n_own - SUB + 1, :], back, 1), b * dims)
        yo_ref[b] = now
        lines.append(
            jnp.concatenate(
                [((yo_ref[b, m : m + brows, :] - c_b) * r_b).astype(jnp.bfloat16) for m in range(steps)],
                axis=1,
            )
        )
    own = jnp.concatenate(lines, axis=0)

    exclusion = M // 4
    sub_i = lax.broadcasted_iota(jnp.int32, (SUB, rows), 0)
    lane_i = lax.broadcasted_iota(jnp.int32, (SUB, rows), 1)
    ahead = sub_i * (seg * per) - (lane_i % brows * per + lane_i // brows)

    def sweep(base, carry):
        after, before = carry
        some = seg // SPLIT
        for b in range(per):
            if b:
                y = pltpu.roll(x_ref[0], LANES - b * dims, 1)
                x_ref[b, : n_x - SUB, :] = shift(y[:-SUB], y[SUB:], b * dims)
            for part in range(0, seg, some):
                lines = []
                for j in range(part, part + some, 2):
                    at = j * SUB
                    c_b = spread_lanes(c_ref[at : at + 2 * SUB, :], b)
                    r_b = spread_lanes(r_ref[at : at + 2 * SUB, :], b)
                    lines.append(
                        jnp.concatenate(
                            [
                                (
                                    (x_ref[b, at + m * SUB : at + (m + 2) * SUB, :] - c_b) * r_b
                                ).astype(jnp.bfloat16)
                                for m in range(steps)
                            ],
                            axis=1,
                        )
                    )
                product = times_t(jnp.concatenate(lines, axis=0), own)
                for j in range(some):
                    p = product[j * SUB : (j + 1) * SUB, :]
                    off = (base + part + j) * per + b - me * rows
                    after = jnp.maximum(after, jnp.where(ahead > exclusion - off, p, -1.0))
                    before = jnp.maximum(before, jnp.where(ahead < -exclusion - off, p, -1.0))
        return after, before

    carry = (jnp.full((SUB, rows), -1.0, jnp.float32),) * 2
    if n_chunks == 1:
        carry = sweep(0, carry)
    else:

        def turn(i, carry):
            base = pl.multiple_of(i * chunk, chunk)
            build(base)
            return sweep(base, carry)

        carry = lax.fori_loop(0, n_chunks, turn, carry)
    for best, out_ref in zip(carry, (after_ref, before_ref)):
        best = jnp.take_along_axis(best, lane_i % per * brows + lane_i // per, axis=1)
        out_ref[...] = 2.0 - 2.0 * jnp.max(best, axis=0, keepdims=True)


def profiles(start, pieces, masks, tail, rows, dims, n_blocks):
    per = LANES // dims
    brows = rows // per
    all_rows = n_blocks * brows
    chunk = min(256, all_rows)
    n_x = chunk + (M // per + 2) * SUB
    out = jax.ShapeDtypeStruct((1, rows), jnp.float32)
    vmem = pl.BlockSpec(memory_space=pltpu.VMEM)
    after, before = pl.pallas_call(
        functools.partial(profile_kernel, (masks, dims, rows, n_blocks)),
        out_shape=(out, out),
        in_specs=[pl.BlockSpec(memory_space=pltpu.SMEM)] + [vmem] * (len(pieces) + 1),
        out_specs=(vmem, vmem),
        scratch_shapes=[
            pltpu.VMEM((all_rows + tail.shape[0] + 2 * SUB, LANES), jnp.float32),
            pltpu.VMEM((per, n_x, LANES), jnp.float32),
            pltpu.VMEM((chunk, LANES), jnp.float32),
            pltpu.VMEM((chunk, LANES), jnp.float32),
            pltpu.VMEM((brows + 3 * SUB, LANES), jnp.float32),
            pltpu.VMEM((per, brows + SUB, LANES), jnp.float32),
        ],
        name="profiles",
    )(
        pltpu.with_memory_space_constraint(start, pltpu.SMEM),
        *[pltpu.with_memory_space_constraint(v, pltpu.VMEM) for v in (*pieces, tail)],
    )
    return after.reshape(rows), before.reshape(rows)


def per_device(record, record_tail, projection, window_start):
    rows, dims = record.shape[0], projection.shape[1]
    n_blocks = lax.axis_size("pb") * lax.axis_size("row")
    p_t = projection.T
    mine, parts = project(record, p_t)
    tail, start = project_loaded(record_tail, parts, window_start)
    bits = n_blocks.bit_length() - 1
    flips = [1 << bit | 1 for bit in reversed(range(1, bits))] + [1]
    pieces, masks = [mine], [(0,)]
    held, held_masks = mine, (0,)
    for flip in flips:
        got = lax.ppermute(held, AXES, [(i, i ^ flip) for i in range(n_blocks)])
        got_masks = tuple(m ^ flip for m in held_masks)
        if len(pieces) == 1:
            got, tail = lax.optimization_barrier((got, tail))
        pieces.append(got)
        masks.append(got_masks)
        if flip != flips[-1]:
            held = jnp.concatenate([held, got], axis=0)
            held_masks = held_masks + got_masks
    return profiles(start, pieces, tuple(masks), tail, rows, dims, n_blocks)


def solution(mesh):
    return jax.shard_map(
        per_device,
        mesh=mesh,
        in_specs=(P(("grp", "pb", "row"), None), P("grp", None), P(), P("grp")),
        out_specs=(P(("grp", "pb", "row")), P(("grp", "pb", "row"))),
        check_vma=False,
    )
```
